32 devices in a mesh: px: 8 (over y, x, core), py: 4 (over z).
Axes of the slice: x: 2, y: 2, z: 4, core: 2. Of those that a mesh axis runs over, the one named last changes fastest.
Arguments:
- velocity: float32 [8, 1024, 1024], P(None, 'px', 'py'), may hold values from -6 to 6
- forcing: bfloat16 [8, 1024, 1024], P(None, 'px', 'py'), may hold values from -6 to 6
- cross_x: bfloat16 [8, 1024, 1024], P(None, 'px', 'py'), may hold values from -1.5 to 1.5
- cross_y: bfloat16 [8, 1024, 1024], P(None, 'px', 'py'), may hold values from -1.5 to 1.5
- inv_x: bfloat16 [8, 1024, 1024], P('px'), may hold values from -1 to 2, as said below
- inv_y: bfloat16 [8, 1024, 1024], P('px'), may hold values from -1 to 2, as said below
Outputs:
- velocity_new: float32 [8, 1024, 1024], P(None, 'px', 'py')
The draws below stay inside these ranges and needn't reach their ends.
Inputs may be any that keep to these rules, and one draw needn't show every extreme that they name: `inv_x`: a dense matrix for each level. `inv_y`: a dense matrix for each level.
All inputs are finite; a program needn't handle non-finite values.
Results may differ from the reference program's by a relative error of at most 0.0052.
Values may be sent and summed in bfloat16 or wider, within the bound.
A program may use at most 64 MiB of HBM per device.

```python
import math
import jax
import jax.numpy as jnp
from jax import lax

NX = 1024
NY = 1024
NZ = 8


def dominant_matrix(key, levels, order):
    key_diag, key_noise = jax.random.split(key)
    diagonal = jax.random.uniform(key_diag, (levels, order), jnp.float32, 0.8, 1.2)
    noise = jax.random.normal(key_noise, (levels, order, order), jnp.float32) * (0.6 / math.sqrt(order))
    identity = jnp.eye(order, dtype=jnp.float32)
    whole = noise * (1.0 - identity) + identity * diagonal[:, :, None]
    return whole.astype(jnp.bfloat16)


def draw_inv_x(key, part):
    return dominant_matrix(jax.random.fold_in(key, 11), NZ, NX)


def draw_inv_y(key, part):
    return dominant_matrix(jax.random.fold_in(key, 23), NZ, NY)


def block_scale(key, shape, shards, low, largest):
    def one(axis_at, parts):
        heights = jax.random.uniform(jax.random.fold_in(jax.random.fold_in(key, 6), axis_at), (parts,), jnp.float32, low / len(shards), largest / len(shards))
        return jnp.repeat(jnp.exp(heights), shape[axis_at] // parts).reshape((-1,) + (1,) * (len(shape) - axis_at - 1))

    factor_of = one(*shards[0])
    for cut in shards[1:]:
        factor_of = factor_of * one(*cut)
    return factor_of


def scatter_about(own_key, dims, scale, reach, cuts=(), kind=jnp.bfloat16):
    values = scale * jax.random.normal(own_key, dims, jnp.float32)
    if cuts:
        values = values * block_scale(own_key, dims, cuts, -0.22, 0.18)
    return jnp.clip(values, -reach, reach).astype(kind)


def setup_inputs(seed: int = 0) -> dict:
    streams_of = jax.random.split(jax.random.key(seed), 7)
    velocity = scatter_about(streams_of[0], (NZ, NX, NY), 1.0, 6.0, ((1, 8), (2, 4)), jnp.float32)
    forcing = scatter_about(streams_of[1], (NZ, NX, NY), 1.0, 6.0, ((1, 8), (2, 4)))
    cross_x = jnp.clip(jax.random.uniform(streams_of[2], (NZ, NX, NY), jnp.float32, -1.5, 1.5) * block_scale(streams_of[2], (NZ, NX, NY), ((1, 8), (2, 4)), -0.4, 0.0), -1.5, 1.5).astype(jnp.bfloat16)
    cross_y = jnp.clip(jax.random.uniform(streams_of[3], (NZ, NX, NY), jnp.float32, -1.5, 1.5) * block_scale(streams_of[3], (NZ, NX, NY), ((1, 8), (2, 4)), -0.4, 0.0), -1.5, 1.5).astype(jnp.bfloat16)
    inv_x = draw_inv_x(jax.random.fold_in(streams_of[6], 71), 0)
    inv_y = draw_inv_y(jax.random.fold_in(streams_of[6], 71), 0)
    return {"velocity": velocity, "forcing": forcing, "cross_x": cross_x, "cross_y": cross_y, "inv_x": inv_x, "inv_y": inv_y}


time_step = 0.25


def reference(velocity, forcing, cross_x, cross_y, inv_x, inv_y):
    x_plus = jnp.roll(velocity, -1, 1)
    x_minus = jnp.roll(velocity, 1, 1)
    y_plus = jnp.roll(velocity, -1, 2)
    y_minus = jnp.roll(velocity, 1, 2)
    z_padded = jnp.pad(velocity, ((1, 1), (0, 0), (0, 0)))
    laplace = x_plus + x_minus + y_plus + y_minus - 4.0 * velocity + z_padded[2:] + z_padded[:-2] - 2.0 * velocity
    slope_x = jnp.pad(0.5 * (x_plus - x_minus), ((1, 1), (0, 0), (0, 0)))
    slope_y = jnp.pad(0.5 * (y_plus - y_minus), ((1, 1), (0, 0), (0, 0)))
    mixed_x = 0.5 * (slope_x[2:] - slope_x[:-2])
    mixed_y = 0.5 * (slope_y[2:] - slope_y[:-2])
    total = laplace + cross_x.astype(jnp.float32) * mixed_x + cross_y.astype(jnp.float32) * mixed_y + forcing.astype(jnp.float32)
    rhs = (time_step * total).astype(jnp.bfloat16)

    def sweep_x(pair):
        inverse, level_rhs = pair
        return jnp.dot(inverse, level_rhs, preferred_element_type=jnp.float32).astype(jnp.bfloat16)

    section_one = lax.map(sweep_x, (inv_x, rhs))

    def sweep_y(pair):
        inverse, level_rhs = pair
        return jnp.dot(level_rhs, inverse.T, preferred_element_type=jnp.float32)

    section_two = lax.map(sweep_y, (inv_y, section_one))
    return velocity + section_two
```

```python
import functools

import jax
import jax.numpy as jnp
from jax import lax
from jax.experimental import pallas as pl
from jax.experimental.pallas import tpu as pltpu
from jax.sharding import PartitionSpec as P

time_step = 0.25


def with_halo(cells, sides, width):
    for axis, dim in sides:
        count = lax.axis_size(axis)
        head = lax.slice_in_dim(cells, 0, width, axis=dim)
        tail = lax.slice_in_dim(cells, cells.shape[dim] - width, cells.shape[dim], axis=dim)
        cells = jnp.concatenate(
            [
                lax.ppermute(tail, axis, [(i, (i + 1) % count) for i in range(count)]),
                cells,
                lax.ppermute(head, axis, [((i + 1) % count, i) for i in range(count)]),
            ],
            axis=dim,
        )
    return cells


def shards(velocity, forcing, cross_x, cross_y, inv_x, inv_y):
    padded = with_halo(velocity, (("px", 1), ("py", 2)), 1)
    x_plus = padded[:, 2:, 1:-1]
    x_minus = padded[:, :-2, 1:-1]
    y_plus = padded[:, 1:-1, 2:]
    y_minus = padded[:, 1:-1, :-2]
    z_padded = jnp.pad(velocity, ((1, 1), (0, 0), (0, 0)))
    laplace = (
        x_plus
        + x_minus
        + y_plus
        + y_minus
        - 4.0 * velocity
        + z_padded[2:]
        + z_padded[:-2]
        - 2.0 * velocity
    )
    slope_x = jnp.pad(0.5 * (x_plus - x_minus), ((1, 1), (0, 0), (0, 0)))
    slope_y = jnp.pad(0.5 * (y_plus - y_minus), ((1, 1), (0, 0), (0, 0)))
    mixed_x = 0.5 * (slope_x[2:] - slope_x[:-2])
    mixed_y = 0.5 * (slope_y[2:] - slope_y[:-2])
    total = (
        laplace
        + cross_x.astype(jnp.float32) * mixed_x
        + cross_y.astype(jnp.float32) * mixed_y
        + forcing.astype(jnp.float32)
    )
    rhs = (time_step * total).astype(jnp.bfloat16)
    section_one = jnp.einsum(
        "lab,lbk->lak",
        inv_x,
        lax.all_to_all(rhs, "px", split_axis=0, concat_axis=1, tiled=True),
        preferred_element_type=jnp.float32,
    ).astype(jnp.bfloat16)
    y_lines = lax.all_to_all(section_one, "py", split_axis=1, concat_axis=2, tiled=True)
    section_two = jnp.einsum("lxb,lab->lxa", y_lines, inv_y, preferred_element_type=jnp.float32)
    settled = lax.all_to_all(
        lax.all_to_all(section_two, "py", split_axis=2, concat_axis=1, tiled=True),
        "px",
        split_axis=1,
        concat_axis=0,
        tiled=True,
    )
    return velocity + settled


def send(src, dst, send_sem, recv_sem, target):
    return pltpu.make_async_remote_copy(
        src_ref=src,
        dst_ref=dst,
        send_sem=send_sem,
        recv_sem=recv_sem,
        device_id=target,
        device_id_type=pl.DeviceIdType.MESH,
    )


def kernel(
    npx,
    npy,
    vel_hbm,
    frc_hbm,
    cx_hbm,
    cy_hbm,
    ix_hbm,
    iy_hbm,
    out,
    vel,
    frc,
    cx,
    cy,
    ix,
    iy,
    x_low,
    x_high,
    y_send,
    y_recv,
    slope_x,
    slope_y,
    lap,
    rhs,
    lines_x,
    one,
    lines_y,
    two,
    back,
    load_sem,
    halo_send,
    halo_recv,
    rhs_send,
    rhs_recv,
    one_send,
    one_recv,
    two_send,
    two_recv,
    out_send,
    out_recv,
    own_sem,
):
    me = lax.axis_index("px")
    my = lax.axis_index("py")
    levels, rows, cols = vel.shape
    part = rows // npy
    pieces = [(vel_hbm, vel), (frc_hbm, frc), (cx_hbm, cx), (cy_hbm, cy), (ix_hbm, ix), (iy_hbm, iy)]
    loads = [pltpu.make_async_copy(a, b, load_sem.at[i]) for i, (a, b) in enumerate(pieces)]
    for load in loads:
        load.start()

    barrier = pltpu.get_barrier_semaphore()
    for step in range(1, npx):
        pl.semaphore_signal(barrier, inc=1, device_id={"px": lax.rem(me + step, npx)}, device_id_type=pl.DeviceIdType.MESH)
    for step in range(1, npy):
        pl.semaphore_signal(barrier, inc=1, device_id={"py": lax.rem(my + step, npy)}, device_id_type=pl.DeviceIdType.MESH)

    loads[0].wait()
    lane = lax.broadcasted_iota(jnp.int32, (rows, 128), 1)

    def gather_face(level, faces):
        first, last = faces
        now = vel[level]
        first = jnp.where(lane == level, now[:, 0:1], first)
        last = jnp.where(lane == level, now[:, cols - 1 : cols], last)
        return first, last

    zero = jnp.zeros((rows, 128), jnp.float32)
    first, last = lax.fori_loop(0, levels, gather_face, (zero, zero))
    y_send[0] = jnp.transpose(first)[:levels]
    y_send[1] = jnp.transpose(last)[:levels]
    pl.semaphore_wait(barrier, npx + npy - 2)

    up_x, down_x = lax.rem(me + 1, npx), lax.rem(me + npx - 1, npx)
    up_y, down_y = lax.rem(my + 1, npy), lax.rem(my + npy - 1, npy)
    halos = [
        send(y_send.at[1], y_recv.at[0], halo_send.at[0], halo_recv.at[0], {"py": up_y}),
        send(y_send.at[0], y_recv.at[1], halo_send.at[1], halo_recv.at[1], {"py": down_y}),
        send(vel.at[:, pl.ds(rows - 8, 8), :], x_low, halo_send.at[2], halo_recv.at[2], {"px": up_x}),
        send(vel.at[:, pl.ds(0, 8), :], x_high, halo_send.at[3], halo_recv.at[3], {"px": down_x}),
    ]
    for halo in halos:
        halo.start()
    for halo in halos:
        halo.wait_recv()

    spare = jnp.zeros((128 - levels, rows), jnp.float32)
    face_low = jnp.transpose(jnp.concatenate([y_recv[0], spare], axis=0))
    face_high = jnp.transpose(jnp.concatenate([y_recv[1], spare], axis=0))
    row_at = lax.broadcasted_iota(jnp.int32, (rows, cols), 0)
    col_at = lax.broadcasted_iota(jnp.int32, (rows, cols), 1)
    blank = jnp.zeros((rows, cols), jnp.float32)
    for edge in (0, levels + 1):
        slope_x[edge] = blank
        slope_y[edge] = blank

    def slopes(level, _):
        now = vel[level]
        low = jnp.sum(jnp.where(lane == level, face_low, 0.0), axis=1, keepdims=True)
        high = jnp.sum(jnp.where(lane == level, face_high, 0.0), axis=1, keepdims=True)
        x_minus = jnp.where(row_at == 0, x_low[level][7:8, :], pltpu.roll(now, 1, 0))
        x_plus = jnp.where(row_at == rows - 1, x_high[level][0:1, :], pltpu.roll(now, rows - 1, 0))
        y_minus = jnp.where(col_at == 0, low, pltpu.roll(now, 1, 1))
        y_plus = jnp.where(col_at == cols - 1, high, pltpu.roll(now, cols - 1, 1))
        slope_x[level + 1] = 0.5 * (x_plus - x_minus)
        slope_y[level + 1] = 0.5 * (y_plus - y_minus)
        lap[level] = x_plus + x_minus + y_plus + y_minus - 4.0 * now
        return 0

    lax.fori_loop(0, levels, slopes, 0)
    for load in loads[1:4]:
        load.wait()

    def right_side(step, _):
        level = lax.rem(me + 1 + step, npx)
        above = jnp.minimum(level + 1, levels - 1)
        below = jnp.maximum(level - 1, 0)
        z_plus = jnp.where(level < levels - 1, 1.0, 0.0) * vel[above]
        z_minus = jnp.where(level > 0, 1.0, 0.0) * vel[below]
        total = lap[level] + z_plus + z_minus - 2.0 * vel[level]
        total += cx[level].astype(jnp.float32) * (0.5 * (slope_x[level + 2] - slope_x[level]))
        total += cy[level].astype(jnp.float32) * (0.5 * (slope_y[level + 2] - slope_y[level]))
        total += frc[level].astype(jnp.float32)
        value = (time_step * total).astype(jnp.bfloat16)

        @pl.when(step < npx - 1)
        def _():
            rhs[level] = value
            send(rhs.at[level], lines_x.at[me], rhs_send.at[level], rhs_recv.at[me], {"px": level}).start()

        @pl.when(step == npx - 1)
        def _():
            lines_x[me] = value

        return 0

    lax.fori_loop(0, npx, right_side, 0)

    def from_px(step):
        other = lax.rem(me + step, npx)
        return send(rhs.at[other], lines_x.at[other], rhs_send.at[other], rhs_recv.at[other], {"px": other})

    loads[4].wait()

    def wait_px(step, _):
        from_px(step).wait_recv()
        return 0

    lax.fori_loop(1, npx, wait_px, 0)

    def cut(at):
        return pl.ds(pl.multiple_of(at * part, part), part)

    def strip(at):
        return pl.ds(pl.multiple_of(at * cols, cols), cols)

    def to_y(step):
        other = lax.rem(my + step, npy)
        return send(one.at[other], lines_y.at[:, :, strip(my)], one_send.at[other], one_recv.at[my], {"py": other})

    order_x = npx * rows
    for step in [2, 1, 3, 0] if npy == 4 else [*range(1, npy), 0]:
        other = lax.rem(my + step, npy)
        mine = ix[:, cut(other), :].reshape(npx * part, order_x)
        value = jnp.dot(mine, lines_x[...].reshape(order_x, cols), preferred_element_type=jnp.float32)
        value = value.astype(jnp.bfloat16).reshape(npx, part, cols)
        if step:
            one[other] = value
            to_y(step).start()
        else:
            lines_y[:, :, strip(my)] = value

    loads[5].wait()
    for step in range(1, npy):
        other = lax.rem(my + step, npy)
        send(one.at[other], lines_y.at[:, :, strip(other)], one_send.at[other], one_recv.at[other], {"py": other}).wait_recv()

    def to_cells(step):
        other = lax.rem(my + step, npy)
        return send(two.at[other], back.at[my], two_send.at[other], two_recv.at[my], {"py": other})

    order_y = npy * cols
    for step in [2, 1, 3, 0] if npy == 4 else [*range(1, npy), 0]:
        other = lax.rem(my + step, npy)
        value = lax.dot_general(
            lines_y[...].reshape(npx * part, order_y),
            iy[strip(other), :],
            (((1,), (1,)), ((), ())),
            preferred_element_type=jnp.float32,
        )
        value = value.astype(jnp.bfloat16).reshape(npx, part, cols)
        if step:
            two[other] = value
            to_cells(step).start()
        else:
            back[my] = value

    def hand_on(origin, step):
        other = lax.rem(me + step, npx)
        return send(
            back.at[origin, other], out.at[me, cut(origin), :], out_send.at[origin, other], out_recv.at[me], {"px": other}
        )

    def own(origin):
        return pltpu.make_async_copy(back.at[origin, me], out.at[me, cut(origin), :], own_sem.at[origin])

    for hop in [0, 1, 3, 2] if npy == 4 else range(npy):
        origin = lax.rem(my + hop, npy)
        if hop:
            send(two.at[origin], back.at[origin], two_send.at[origin], two_recv.at[origin], {"py": origin}).wait_recv()

        def give(step, _):
            hand_on(origin, step).start()
            return 0

        lax.fori_loop(1, npx, give, 0)
        own(origin).start()

    def settle(step, _):
        other = lax.rem(me + step, npx)
        send(rhs.at[other], out.at[other], rhs_send.at[other], out_recv.at[other], {"px": other}).wait_recv()
        from_px(step).wait_send()
        return 0

    lax.fori_loop(1, npx, settle, 0)
    for halo in halos:
        halo.wait_send()
    for step in range(1, npy):
        to_y(step).wait_send()
        to_cells(step).wait_send()
    for hop in range(npy):
        origin = lax.rem(my + hop, npy)
        own(origin).wait()

        def sent(step, _):
            hand_on(origin, step).wait_send()
            return 0

        lax.fori_loop(1, npx, sent, 0)


def fused(velocity, forcing, cross_x, cross_y, inv_x, inv_y):
    npx, npy = lax.axis_size("px"), lax.axis_size("py")
    levels, rows, cols = velocity.shape
    part = rows // npy
    shape, narrow = velocity.shape, jnp.bfloat16
    order_x, order_y = npx * rows, npy * cols
    vmem, dma = pltpu.VMEM, pltpu.SemaphoreType.DMA
    settled = pl.pallas_call(
        functools.partial(kernel, npx, npy),
        out_shape=jax.ShapeDtypeStruct(shape, narrow),
        in_specs=[pl.BlockSpec(memory_space=pl.ANY)] * 6,
        out_specs=pl.BlockSpec(memory_space=pl.ANY),
        scratch_shapes=[
            vmem(shape, jnp.float32),
            vmem(shape, narrow),
            vmem(shape, narrow),
            vmem(shape, narrow),
            vmem((npx, rows, order_x), narrow),
            vmem((order_y, order_y), narrow),
            vmem((levels, 8, cols), jnp.float32),
            vmem((levels, 8, cols), jnp.float32),
            vmem((2, levels, rows), jnp.float32),
            vmem((2, levels, rows), jnp.float32),
            vmem((levels + 2, rows, cols), jnp.float32),
            vmem((levels + 2, rows, cols), jnp.float32),
            vmem(shape, jnp.float32),
            vmem(shape, narrow),
            vmem((npx, rows, cols), narrow),
            vmem((npy, npx, part, cols), narrow),
            vmem((npx, part, order_y), narrow),
            vmem((npy, npx, part, cols), narrow),
            vmem((npy, npx, part, cols), narrow),
            dma((6,)),
            dma((4,)),
            dma((4,)),
            dma((npx,)),
            dma((npx,)),
            dma((npy,)),
            dma((npy,)),
            dma((npy,)),
            dma((npy,)),
            dma((npy, npx)),
            dma((npx,)),
            dma((npy,)),
        ],
        compiler_params=pltpu.CompilerParams(collective_id=0, has_side_effects=True, vmem_limit_bytes=48 * 1024 * 1024),
        cost_estimate=pl.CostEstimate(flops=4 * order_x * order_y * rows, bytes_accessed=8 * 1024 * 1024, transcendentals=0),
    )(
        velocity,
        forcing,
        cross_x,
        cross_y,
        inv_x.reshape(npx, rows, order_x),
        inv_y.reshape(order_y, order_y),
    )
    return velocity + settled.astype(jnp.float32)


def step(velocity, forcing, cross_x, cross_y, inv_x, inv_y):
    npx, npy = lax.axis_size("px"), lax.axis_size("py")
    levels, rows, cols = velocity.shape
    aligned = rows % (16 * npy) == 0 and rows % 128 == 0 and cols % 128 == 0 and levels % 8 == 0
    if aligned and levels == npx and levels <= 128 and inv_x.shape[0] == 1:
        return fused(velocity, forcing, cross_x, cross_y, inv_x, inv_y)
    return shards(velocity, forcing, cross_x, cross_y, inv_x, inv_y)


def solution(mesh):
    return jax.shard_map(
        step,
        mesh=mesh,
        in_specs=(
            P(None, "px", "py"),
            P(None, "px", "py"),
            P(None, "px", "py"),
            P(None, "px", "py"),
            P("px", None, None),
            P("px", None, None),
        ),
        out_specs=P(None, "px", "py"),
        check_vma=False,
    )
```

```python
import functools

import jax
import jax.numpy as jnp
from jax import lax
from jax.experimental import pallas as pl
from jax.experimental.pallas import tpu as pltpu
from jax.sharding import PartitionSpec as P

time_step = 0.25


def with_halo(cells, sides, width):
    for axis, dim in sides:
        count = lax.axis_size(axis)
        head = lax.slice_in_dim(cells, 0, width, axis=dim)
        tail = lax.slice_in_dim(cells, cells.shape[dim] - width, cells.shape[dim], axis=dim)
        cells = jnp.concatenate(
            [
                lax.ppermute(tail, axis, [(i, (i + 1) % count) for i in range(count)]),
                cells,
                lax.ppermute(head, axis, [((i + 1) % count, i) for i in range(count)]),
            ],
            axis=dim,
        )
    return cells


def shards(velocity, forcing, cross_x, cross_y, inv_x, inv_y):
    padded = with_halo(velocity, (("px", 1), ("py", 2)), 1)
    x_plus = padded[:, 2:, 1:-1]
    x_minus = padded[:, :-2, 1:-1]
    y_plus = padded[:, 1:-1, 2:]
    y_minus = padded[:, 1:-1, :-2]
    z_padded = jnp.pad(velocity, ((1, 1), (0, 0), (0, 0)))
    laplace = (
        x_plus
        + x_minus
        + y_plus
        + y_minus
        - 4.0 * velocity
        + z_padded[2:]
        + z_padded[:-2]
        - 2.0 * velocity
    )
    slope_x = jnp.pad(0.5 * (x_plus - x_minus), ((1, 1), (0, 0), (0, 0)))
    slope_y = jnp.pad(0.5 * (y_plus - y_minus), ((1, 1), (0, 0), (0, 0)))
    mixed_x = 0.5 * (slope_x[2:] - slope_x[:-2])
    mixed_y = 0.5 * (slope_y[2:] - slope_y[:-2])
    total = (
        laplace
        + cross_x.astype(jnp.float32) * mixed_x
        + cross_y.astype(jnp.float32) * mixed_y
        + forcing.astype(jnp.float32)
    )
    rhs = (time_step * total).astype(jnp.bfloat16)
    section_one = jnp.einsum(
        "lab,lbk->lak",
        inv_x,
        lax.all_to_all(rhs, "px", split_axis=0, concat_axis=1, tiled=True),
        preferred_element_type=jnp.float32,
    ).astype(jnp.bfloat16)
    y_lines = lax.all_to_all(section_one, "py", split_axis=1, concat_axis=2, tiled=True)
    section_two = jnp.einsum("lxb,lab->lxa", y_lines, inv_y, preferred_element_type=jnp.float32)
    settled = lax.all_to_all(
        lax.all_to_all(section_two, "py", split_axis=2, concat_axis=1, tiled=True),
        "px",
        split_axis=1,
        concat_axis=0,
        tiled=True,
    )
    return velocity + settled


def send(src, dst, send_sem, recv_sem, target):
    return pltpu.make_async_remote_copy(
        src_ref=src,
        dst_ref=dst,
        send_sem=send_sem,
        recv_sem=recv_sem,
        device_id=target,
        device_id_type=pl.DeviceIdType.MESH,
    )


def kernel(
    npx,
    npy,
    vel_hbm,
    frc_hbm,
    cx_hbm,
    cy_hbm,
    ix_hbm,
    iy_hbm,
    out,
    vel,
    frc,
    cx,
    cy,
    ix,
    iy,
    x_low,
    x_high,
    y_send,
    y_recv,
    slope_x,
    slope_y,
    lap,
    rhs,
    lines_x,
    one,
    lines_y,
    two,
    back,
    load_sem,
    halo_send,
    halo_recv,
    rhs_send,
    rhs_recv,
    one_send,
    one_recv,
    two_send,
    two_recv,
    out_send,
    out_recv,
    own_sem,
):
    me = lax.axis_index("px")
    my = lax.axis_index("py")
    levels, rows, cols = vel.shape
    part = rows // npy
    chunks = rhs.shape[0]
    wide = cols // chunks
    pieces = [(vel_hbm, vel), (frc_hbm, frc), (cx_hbm, cx), (cy_hbm, cy), (ix_hbm, ix), (iy_hbm, iy)]
    loads = [pltpu.make_async_copy(a, b, load_sem.at[i]) for i, (a, b) in enumerate(pieces)]
    for load in loads:
        load.start()

    barrier = pltpu.get_barrier_semaphore()
    for step in range(1, npx):
        pl.semaphore_signal(barrier, inc=1, device_id={"px": lax.rem(me + step, npx)}, device_id_type=pl.DeviceIdType.MESH)
    for step in range(1, npy):
        pl.semaphore_signal(barrier, inc=1, device_id={"py": lax.rem(my + step, npy)}, device_id_type=pl.DeviceIdType.MESH)

    loads[0].wait()
    lane = lax.broadcasted_iota(jnp.int32, (rows, 128), 1)

    def gather_face(level, faces):
        first, last = faces
        now = vel[level]
        first = jnp.where(lane == level, now[:, 0:1], first)
        last = jnp.where(lane == level, now[:, cols - 1 : cols], last)
        return first, last

    zero = jnp.zeros((rows, 128), jnp.float32)
    first, last = lax.fori_loop(0, levels, gather_face, (zero, zero))
    y_send[0] = jnp.transpose(first)[:levels]
    y_send[1] = jnp.transpose(last)[:levels]
    pl.semaphore_wait(barrier, npx + npy - 2)

    up_x, down_x = lax.rem(me + 1, npx), lax.rem(me + npx - 1, npx)
    up_y, down_y = lax.rem(my + 1, npy), lax.rem(my + npy - 1, npy)
    halos = [
        send(y_send.at[1], y_recv.at[0], halo_send.at[0], halo_recv.at[0], {"py": up_y}),
        send(y_send.at[0], y_recv.at[1], halo_send.at[1], halo_recv.at[1], {"py": down_y}),
        send(vel.at[:, pl.ds(rows - 8, 8), :], x_low, halo_send.at[2], halo_recv.at[2], {"px": up_x}),
        send(vel.at[:, pl.ds(0, 8), :], x_high, halo_send.at[3], halo_recv.at[3], {"px": down_x}),
    ]
    for halo in halos:
        halo.start()
    for halo in halos:
        halo.wait_recv()

    spare = jnp.zeros((128 - levels, rows), jnp.float32)
    face_low = jnp.transpose(jnp.concatenate([y_recv[0], spare], axis=0))
    face_high = jnp.transpose(jnp.concatenate([y_recv[1], spare], axis=0))
    row_at = lax.broadcasted_iota(jnp.int32, (rows, cols), 0)
    col_at = lax.broadcasted_iota(jnp.int32, (rows, cols), 1)
    blank = jnp.zeros((rows, cols), jnp.float32)
    for edge in (0, levels + 1):
        slope_x[edge] = blank
        slope_y[edge] = blank

    def slopes(level, _):
        now = vel[level]
        low = jnp.sum(jnp.where(lane == level, face_low, 0.0), axis=1, keepdims=True)
        high = jnp.sum(jnp.where(lane == level, face_high, 0.0), axis=1, keepdims=True)
        x_minus = jnp.where(row_at == 0, x_low[level][7:8, :], pltpu.roll(now, 1, 0))
        x_plus = jnp.where(row_at == rows - 1, x_high[level][0:1, :], pltpu.roll(now, rows - 1, 0))
        y_minus = jnp.where(col_at == 0, low, pltpu.roll(now, 1, 1))
        y_plus = jnp.where(col_at == cols - 1, high, pltpu.roll(now, cols - 1, 1))
        slope_x[level + 1] = 0.5 * (x_plus - x_minus)
        slope_y[level + 1] = 0.5 * (y_plus - y_minus)
        lap[level] = x_plus + x_minus + y_plus + y_minus - 4.0 * now
        return 0

    lax.fori_loop(0, levels, slopes, 0)
    for load in loads[1:4]:
        load.wait()

    def right_side(chunk, at):
        level = lax.rem(me + 1 + at, npx)
        side = slice(chunk * wide, (chunk + 1) * wide)
        above = jnp.minimum(level + 1, levels - 1)
        below = jnp.maximum(level - 1, 0)
        z_plus = jnp.where(level < levels - 1, 1.0, 0.0) * vel[above, :, side]
        z_minus = jnp.where(level > 0, 1.0, 0.0) * vel[below, :, side]
        total = lap[level, :, side] + z_plus + z_minus - 2.0 * vel[level, :, side]
        total += cx[level, :, side].astype(jnp.float32) * (0.5 * (slope_x[level + 2, :, side] - slope_x[level, :, side]))
        total += cy[level, :, side].astype(jnp.float32) * (0.5 * (slope_y[level + 2, :, side] - slope_y[level, :, side]))
        total += frc[level, :, side].astype(jnp.float32)
        value = (time_step * total).astype(jnp.bfloat16)

        @pl.when(at < npx - 1)
        def _():
            rhs[chunk, level] = value
            to_px(chunk, level).start()

        @pl.when(at == npx - 1)
        def _():
            lines_x[chunk, me] = value

    def to_px(chunk, other):
        return send(
            rhs.at[chunk, other], lines_x.at[chunk, me], rhs_send.at[chunk, other], rhs_recv.at[chunk, me], {"px": other}
        )

    def from_px(chunk, other):
        return send(
            rhs.at[chunk, other], lines_x.at[chunk, other], rhs_send.at[chunk, other], rhs_recv.at[chunk, other], {"px": other}
        )

    def over_px(body):
        def one_step(at, _):
            body(lax.rem(me + at, npx))
            return 0

        lax.fori_loop(1, npx, one_step, 0)

    for chunk in range(chunks):
        def one_level(at, _):
            right_side(chunk, at)
            return 0

        lax.fori_loop(0, npx, one_level, 0)

    half = part // 2
    forward = [(chunk, 0, part) for chunk in range(chunks - 1)] + [(chunks - 1, 0, half), (chunks - 1, half, half)]
    order = [2, 1, 3, 0] if npy == 4 else [*range(1, npy), 0]
    order_x, order_y = npx * rows, npy * cols

    def strip(at, chunk=0, width=cols):
        return pl.ds(pl.multiple_of(at * cols + chunk * wide, wide), width)

    def piece_y(index, other, source):
        chunk, first, count = forward[index]
        return send(
            one.at[index, other, :, pl.ds(0, count)],
            lines_y.at[:, pl.ds(first, count), strip(source, chunk, wide)],
            one_send.at[index, other],
            one_recv.at[index, source],
            {"py": other},
        )

    loads[4].wait()
    for index, (chunk, first, count) in enumerate(forward):
        if first == 0:
            over_px(lambda other: from_px(chunk, other).wait_recv())
        for step in order:
            other = lax.rem(my + step, npy)
            mine = ix[:, pl.ds(pl.multiple_of(other * part + first, half), count), :].reshape(npx * count, order_x)
            value = jnp.dot(mine, lines_x[chunk].reshape(order_x, wide), preferred_element_type=jnp.float32)
            value = value.astype(jnp.bfloat16).reshape(npx, count, wide)
            if step:
                one[index, other, :, 0:count] = value
                piece_y(index, other, my).start()
            else:
                lines_y[:, first : first + count, strip(my, chunk, wide)] = value

    def piece_back(side, other, source):
        return send(two.at[side, other], back.at[side, source], two_send.at[side, other], two_recv.at[side, source], {"py": other})

    def cut(side, origin):
        return pl.ds(pl.multiple_of(origin * part + side * half, half), half)

    def hand_on(side, origin, other):
        return send(
            back.at[side, origin, other],
            out.at[me, cut(side, origin), :],
            out_send.at[side, origin, other],
            out_recv.at[me],
            {"px": other},
        )

    def own(side, origin):
        return pltpu.make_async_copy(back.at[side, origin, me], out.at[me, cut(side, origin), :], own_sem.at[side, origin])

    loads[5].wait()
    for side in range(2):
        for index, (chunk, first, count) in enumerate(forward):
            if first == side * half and (side == 1 or count > 0):
                for step in range(1, npy):
                    source = lax.rem(my + step, npy)
                    piece_y(index, source, source).wait_recv()
        held = lines_y[:, side * half : (side + 1) * half, :].reshape(npx * half, order_y)
        for step in order:
            other = lax.rem(my + step, npy)
            value = lax.dot_general(held, iy[strip(other), :], (((1,), (1,)), ((), ())), preferred_element_type=jnp.float32)
            value = value.astype(jnp.bfloat16).reshape(npx, half, cols)
            if step:
                two[side, other] = value
                piece_back(side, other, my).start()
            else:
                back[side, my] = value

    for side in range(2):
        for hop in [0, 1, 3, 2] if npy == 4 else range(npy):
            origin = lax.rem(my + hop, npy)
            if hop:
                piece_back(side, origin, origin).wait_recv()
            over_px(lambda other: hand_on(side, origin, other).start())
            own(side, origin).start()

    def settle(other):
        whole = send(out.at[other], out.at[other], rhs_send.at[0, other], out_recv.at[other], {"px": other})
        whole.wait_recv()
        for chunk in range(chunks):
            to_px(chunk, other).wait_send()

    over_px(settle)
    for halo in halos:
        halo.wait_send()
    for step in range(1, npy):
        other = lax.rem(my + step, npy)
        for index in range(len(forward)):
            piece_y(index, other, my).wait_send()
        for side in range(2):
            piece_back(side, other, my).wait_send()
    for side in range(2):
        for hop in range(npy):
            origin = lax.rem(my + hop, npy)
            own(side, origin).wait()
            over_px(lambda other: hand_on(side, origin, other).wait_send())


def fused(velocity, forcing, cross_x, cross_y, inv_x, inv_y):
    npx, npy = lax.axis_size("px"), lax.axis_size("py")
    levels, rows, cols = velocity.shape
    part = rows // npy
    half, chunks = part // 2, cols // 128
    wide = cols // chunks
    shape, narrow = velocity.shape, jnp.bfloat16
    order_x, order_y = npx * rows, npy * cols
    vmem, dma = pltpu.VMEM, pltpu.SemaphoreType.DMA
    settled = pl.pallas_call(
        functools.partial(kernel, npx, npy),
        out_shape=jax.ShapeDtypeStruct(shape, narrow),
        in_specs=[pl.BlockSpec(memory_space=pl.ANY)] * 6,
        out_specs=pl.BlockSpec(memory_space=pl.ANY),
        scratch_shapes=[
            vmem(shape, jnp.float32),
            vmem(shape, narrow),
            vmem(shape, narrow),
            vmem(shape, narrow),
            vmem((npx, rows, order_x), narrow),
            vmem((order_y, order_y), narrow),
            vmem((levels, 8, cols), jnp.float32),
            vmem((levels, 8, cols), jnp.float32),
            vmem((2, levels, rows), jnp.float32),
            vmem((2, levels, rows), jnp.float32),
            vmem((levels + 2, rows, cols), jnp.float32),
            vmem((levels + 2, rows, cols), jnp.float32),
            vmem(shape, jnp.float32),
            vmem((chunks, levels, rows, wide), narrow),
            vmem((chunks, npx, rows, wide), narrow),
            vmem((chunks + 1, npy, npx, part, wide), narrow),
            vmem((npx, part, order_y), narrow),
            vmem((2, npy, npx, half, cols), narrow),
            vmem((2, npy, npx, half, cols), narrow),
            dma((6,)),
            dma((4,)),
            dma((4,)),
            dma((chunks, npx)),
            dma((chunks, npx)),
            dma((chunks + 1, npy)),
            dma((chunks + 1, npy)),
            dma((2, npy)),
            dma((2, npy)),
            dma((2, npy, npx)),
            dma((npx,)),
            dma((2, npy)),
        ],
        compiler_params=pltpu.CompilerParams(collective_id=0, has_side_effects=True, vmem_limit_bytes=67_043_328),
        cost_estimate=pl.CostEstimate(flops=4 * order_x * order_y * rows, bytes_accessed=8 * 1024 * 1024, transcendentals=0),
    )(
        velocity,
        forcing,
        cross_x,
        cross_y,
        inv_x.reshape(npx, rows, order_x),
        inv_y.reshape(order_y, order_y),
    )
    return velocity + settled.astype(jnp.float32)


def step(velocity, forcing, cross_x, cross_y, inv_x, inv_y):
    npx, npy = lax.axis_size("px"), lax.axis_size("py")
    levels, rows, cols = velocity.shape
    aligned = rows % (32 * npy) == 0 and rows % 128 == 0 and cols % 128 == 0 and levels % 8 == 0
    if aligned and levels == npx and levels <= 128 and inv_x.shape[0] == 1:
        return fused(velocity, forcing, cross_x, cross_y, inv_x, inv_y)
    return shards(velocity, forcing, cross_x, cross_y, inv_x, inv_y)


def solution(mesh):
    return jax.shard_map(
        step,
        mesh=mesh,
        in_specs=(
            P(None, "px", "py"),
            P(None, "px", "py"),
            P(None, "px", "py"),
            P(None, "px", "py"),
            P("px", None, None),
            P("px", None, None),
        ),
        out_specs=P(None, "px", "py"),
        check_vma=False,
    )
```

```python
import functools

import jax
import jax.numpy as jnp
from jax import lax
from jax.experimental import pallas as pl
from jax.experimental.pallas import tpu as pltpu
from jax.sharding import PartitionSpec as P

time_step = 0.25


def with_halo(cells, sides, width):
    for axis, dim in sides:
        count = lax.axis_size(axis)
        head = lax.slice_in_dim(cells, 0, width, axis=dim)
        tail = lax.slice_in_dim(cells, cells.shape[dim] - width, cells.shape[dim], axis=dim)
        cells = jnp.concatenate(
            [
                lax.ppermute(tail, axis, [(i, (i + 1) % count) for i in range(count)]),
                cells,
                lax.ppermute(head, axis, [((i + 1) % count, i) for i in range(count)]),
            ],
            axis=dim,
        )
    return cells


def shards(velocity, forcing, cross_x, cross_y, inv_x, inv_y):
    padded = with_halo(velocity, (("px", 1), ("py", 2)), 1)
    x_plus = padded[:, 2:, 1:-1]
    x_minus = padded[:, :-2, 1:-1]
    y_plus = padded[:, 1:-1, 2:]
    y_minus = padded[:, 1:-1, :-2]
    z_padded = jnp.pad(velocity, ((1, 1), (0, 0), (0, 0)))
    laplace = (
        x_plus
        + x_minus
        + y_plus
        + y_minus
        - 4.0 * velocity
        + z_padded[2:]
        + z_padded[:-2]
        - 2.0 * velocity
    )
    slope_x = jnp.pad(0.5 * (x_plus - x_minus), ((1, 1), (0, 0), (0, 0)))
    slope_y = jnp.pad(0.5 * (y_plus - y_minus), ((1, 1), (0, 0), (0, 0)))
    mixed_x = 0.5 * (slope_x[2:] - slope_x[:-2])
    mixed_y = 0.5 * (slope_y[2:] - slope_y[:-2])
    total = (
        laplace
        + cross_x.astype(jnp.float32) * mixed_x
        + cross_y.astype(jnp.float32) * mixed_y
        + forcing.astype(jnp.float32)
    )
    rhs = (time_step * total).astype(jnp.bfloat16)
    section_one = jnp.einsum(
        "lab,lbk->lak",
        inv_x,
        lax.all_to_all(rhs, "px", split_axis=0, concat_axis=1, tiled=True),
        preferred_element_type=jnp.float32,
    ).astype(jnp.bfloat16)
    y_lines = lax.all_to_all(section_one, "py", split_axis=1, concat_axis=2, tiled=True)
    section_two = jnp.einsum("lxb,lab->lxa", y_lines, inv_y, preferred_element_type=jnp.float32)
    settled = lax.all_to_all(
        lax.all_to_all(section_two, "py", split_axis=2, concat_axis=1, tiled=True),
        "px",
        split_axis=1,
        concat_axis=0,
        tiled=True,
    )
    return velocity + settled


def send(src, dst, send_sem, recv_sem, target):
    return pltpu.make_async_remote_copy(
        src_ref=src,
        dst_ref=dst,
        send_sem=send_sem,
        recv_sem=recv_sem,
        device_id=target,
        device_id_type=pl.DeviceIdType.MESH,
    )


def kernel(
    npx,
    npy,
    vel_hbm,
    frc_hbm,
    cx_hbm,
    cy_hbm,
    ix_hbm,
    iy_hbm,
    out,
    vel,
    frc,
    cx,
    cy,
    ix,
    iy,
    x_low,
    x_high,
    y_send,
    y_recv,
    slope_x,
    slope_y,
    lap,
    rhs,
    lines_x,
    one,
    lines_y,
    two,
    back,
    load_sem,
    halo_send,
    halo_recv,
    rhs_send,
    rhs_recv,
    one_send,
    one_recv,
    two_send,
    two_recv,
    out_send,
    out_recv,
    own_sem,
):
    me = lax.axis_index("px")
    my = lax.axis_index("py")
    levels, rows, cols = vel.shape
    part = rows // npy
    chunks = rhs.shape[0]
    wide = cols // chunks
    pieces = [(vel_hbm, vel), (frc_hbm, frc), (cx_hbm, cx), (cy_hbm, cy), (ix_hbm, ix), (iy_hbm, iy)]
    loads = [pltpu.make_async_copy(a, b, load_sem.at[i]) for i, (a, b) in enumerate(pieces)]
    loads[0].start()

    barrier = pltpu.get_barrier_semaphore()
    for step in range(1, npx):
        pl.semaphore_signal(barrier, inc=1, device_id={"px": lax.rem(me + step, npx)}, device_id_type=pl.DeviceIdType.MESH)
    for step in range(1, npy):
        pl.semaphore_signal(barrier, inc=1, device_id={"py": lax.rem(my + step, npy)}, device_id_type=pl.DeviceIdType.MESH)

    loads[0].wait()
    for load in loads[1:]:
        load.start()
    lane = lax.broadcasted_iota(jnp.int32, (rows, 128), 1)

    def gather_face(level, faces):
        first, last = faces
        now = vel[level]
        first = jnp.where(lane == level, now[:, 0:1], first)
        last = jnp.where(lane == level, now[:, cols - 1 : cols], last)
        return first, last

    zero = jnp.zeros((rows, 128), jnp.float32)
    first, last = lax.fori_loop(0, levels, gather_face, (zero, zero))
    y_send[0] = jnp.transpose(first)[:levels]
    y_send[1] = jnp.transpose(last)[:levels]
    pl.semaphore_wait(barrier, npx + npy - 2)

    up_x, down_x = lax.rem(me + 1, npx), lax.rem(me + npx - 1, npx)
    up_y, down_y = lax.rem(my + 1, npy), lax.rem(my + npy - 1, npy)
    halos = [
        send(y_send.at[1], y_recv.at[0], halo_send.at[0], halo_recv.at[0], {"py": up_y}),
        send(y_send.at[0], y_recv.at[1], halo_send.at[1], halo_recv.at[1], {"py": down_y}),
        send(vel.at[:, pl.ds(rows - 8, 8), :], x_low, halo_send.at[2], halo_recv.at[2], {"px": up_x}),
        send(vel.at[:, pl.ds(0, 8), :], x_high, halo_send.at[3], halo_recv.at[3], {"px": down_x}),
    ]
    for halo in halos:
        halo.start()
    row_at = lax.broadcasted_iota(jnp.int32, (rows, cols), 0)
    col_at = lax.broadcasted_iota(jnp.int32, (rows, cols), 1)
    blank = jnp.zeros((rows, cols), jnp.float32)
    for edge in (0, levels + 1):
        slope_x[edge] = blank
        slope_y[edge] = blank

    def slopes(level, _):
        now = vel[level]
        x_minus = jnp.where(row_at == 0, 0.0, pltpu.roll(now, 1, 0))
        x_plus = jnp.where(row_at == rows - 1, 0.0, pltpu.roll(now, rows - 1, 0))
        y_minus = jnp.where(col_at == 0, 0.0, pltpu.roll(now, 1, 1))
        y_plus = jnp.where(col_at == cols - 1, 0.0, pltpu.roll(now, cols - 1, 1))
        slope_x[level + 1] = 0.5 * (x_plus - x_minus)
        slope_y[level + 1] = 0.5 * (y_plus - y_minus)
        lap[level] = x_plus + x_minus + y_plus + y_minus - 4.0 * now
        return 0

    lax.fori_loop(0, levels, slopes, 0)
    for load in loads[1:4]:
        load.wait()

    def inner(level, _):
        above = jnp.minimum(level + 1, levels - 1)
        below = jnp.maximum(level - 1, 0)
        z_plus = jnp.where(level < levels - 1, 1.0, 0.0) * vel[above]
        z_minus = jnp.where(level > 0, 1.0, 0.0) * vel[below]
        total = lap[level] + z_plus + z_minus - 2.0 * vel[level]
        total += cx[level].astype(jnp.float32) * (0.5 * (slope_x[level + 2] - slope_x[level]))
        total += cy[level].astype(jnp.float32) * (0.5 * (slope_y[level + 2] - slope_y[level]))
        lap[level] = total + frc[level].astype(jnp.float32)
        return 0

    lax.fori_loop(0, levels, inner, 0)
    for halo in halos:
        halo.wait_recv()

    def level_slope(face, axis, at):
        size = face.shape[axis]
        lower = jnp.where(at == 0, 0.0, pltpu.roll(face, 1, axis))
        upper = jnp.where(at == levels - 1, 0.0, pltpu.roll(face, size - 1, axis))
        return 0.25 * (upper - lower)

    spare = jnp.zeros((128 - levels, rows), jnp.float32)
    face_low = jnp.transpose(jnp.concatenate([y_recv[0], spare], axis=0))
    face_high = jnp.transpose(jnp.concatenate([y_recv[1], spare], axis=0))
    mixed_low = -level_slope(face_low, 1, lane)
    mixed_high = level_slope(face_high, 1, lane)
    level_at = lax.broadcasted_iota(jnp.int32, (levels, cols), 0)
    x_face = (x_low[:, 7, :], x_high[:, 0, :])
    x_mixed = (-level_slope(x_face[0], 0, level_at), level_slope(x_face[1], 0, level_at))
    slab_at = lax.broadcasted_iota(jnp.int32, (16, wide), 0)
    wide_at = lax.broadcasted_iota(jnp.int32, (rows, wide), 1)

    def right_side(chunk, at):
        level = lax.rem(me + 1 + at, npx)
        side = slice(chunk * wide, (chunk + 1) * wide)

        def row(faces):
            return jnp.sum(jnp.where(level_at[:, side] == level, faces, 0.0), axis=0, keepdims=True)

        for end, first in enumerate((0, rows - 16)):
            slab = slice(first, first + 16)
            face = row(x_face[end][:, side]) + cx[level, slab, side].astype(jnp.float32) * row(x_mixed[end][:, side])
            lap[level, slab, side] += jnp.where(slab_at == 15 * end, face, 0.0)
        total = lap[level, :, side]

        def column(faces):
            return jnp.sum(jnp.where(lane == level, faces, 0.0), axis=1, keepdims=True)

        for at_chunk, at_col, faces, mixed in ((0, 0, face_low, mixed_low), (chunks - 1, wide - 1, face_high, mixed_high)):
            if chunk == at_chunk:
                face = column(faces) + cy[level, :, side].astype(jnp.float32) * column(mixed)
                total += jnp.where(wide_at == at_col, face, 0.0)
        value = (time_step * total).astype(jnp.bfloat16)

        @pl.when(at < npx - 1)
        def _():
            rhs[chunk, level] = value
            to_px(chunk, level).start()

        @pl.when(at == npx - 1)
        def _():
            lines_x[chunk, me] = value

    def to_px(chunk, other):
        return send(
            rhs.at[chunk, other], lines_x.at[chunk, me], rhs_send.at[chunk, other], rhs_recv.at[chunk, me], {"px": other}
        )

    def from_px(chunk, other):
        return send(
            rhs.at[chunk, other], lines_x.at[chunk, other], rhs_send.at[chunk, other], rhs_recv.at[chunk, other], {"px": other}
        )

    def over_px(body):
        def one_step(at, _):
            body(lax.rem(me + at, npx))
            return 0

        lax.fori_loop(1, npx, one_step, 0)

    for chunk in range(chunks):
        def one_level(at, _):
            right_side(chunk, at)
            return 0

        lax.fori_loop(0, npx, one_level, 0)

    half = part // 2
    forward = [(chunk, 0, part) for chunk in range(chunks - 1)] + [(chunks - 1, 0, half), (chunks - 1, half, half)]
    order = [*range(1, npy), 0]
    turn = jnp.where(my < npy // 2, 1, npy - 1)

    def mate(step):
        return lax.rem(my + step * turn, npy)

    order_x, order_y = npx * rows, npy * cols

    def strip(at, chunk=0, width=cols):
        return pl.ds(pl.multiple_of(at * cols + chunk * wide, wide), width)

    def piece_y(index, other, source):
        chunk, first, count = forward[index]
        return send(
            one.at[index, other, :, pl.ds(0, count)],
            lines_y.at[:, pl.ds(first, count), strip(source, chunk, wide)],
            one_send.at[index, other],
            one_recv.at[index, source],
            {"py": other},
        )

    loads[4].wait()
    for index, (chunk, first, count) in enumerate(forward):
        if first == 0:
            over_px(lambda other: from_px(chunk, other).wait_recv())
        for step in order:
            other = mate(step)
            mine = ix[:, pl.ds(pl.multiple_of(other * part + first, half), count), :].reshape(npx * count, order_x)
            value = jnp.dot(mine, lines_x[chunk].reshape(order_x, wide), preferred_element_type=jnp.float32)
            value = value.astype(jnp.bfloat16).reshape(npx, count, wide)
            if step:
                one[index, other, :, 0:count] = value
                piece_y(index, other, my).start()
            else:
                lines_y[:, first : first + count, strip(my, chunk, wide)] = value

    def piece_back(side, other, source):
        return send(two.at[side, other], back.at[side, source], two_send.at[side, other], two_recv.at[side, source], {"py": other})

    def cut(side, origin):
        return pl.ds(pl.multiple_of(origin * part + side * half, half), half)

    def hand_on(side, origin, other):
        return send(
            back.at[side, origin, other],
            out.at[me, cut(side, origin), :],
            out_send.at[side, origin, other],
            out_recv.at[me],
            {"px": other},
        )

    def own(side, origin):
        return pltpu.make_async_copy(back.at[side, origin, me], out.at[me, cut(side, origin), :], own_sem.at[side, origin])

    loads[5].wait()
    for side in range(2):
        for index, (chunk, first, count) in enumerate(forward):
            if first == side * half and (side == 1 or count > 0):
                for step in range(1, npy):
                    source = lax.rem(my + step, npy)
                    piece_y(index, source, source).wait_recv()
        held = lines_y[:, side * half : (side + 1) * half, :].reshape(npx * half, order_y)
        for step in order:
            other = mate(step)
            value = lax.dot_general(held, iy[strip(other), :], (((1,), (1,)), ((), ())), preferred_element_type=jnp.float32)
            value = value.astype(jnp.bfloat16).reshape(npx, half, cols)
            if step:
                two[side, other] = value
                piece_back(side, other, my).start()
            else:
                back[side, my] = value

    for side in range(2):
        for hop in [0, 1, 3, 2] if npy == 4 else range(npy):
            origin = lax.rem(my + hop, npy)
            if hop:
                piece_back(side, origin, origin).wait_recv()
            over_px(lambda other: hand_on(side, origin, other).start())
            own(side, origin).start()

    def settle(other):
        whole = send(out.at[other], out.at[other], rhs_send.at[0, other], out_recv.at[other], {"px": other})
        whole.wait_recv()
        for chunk in range(chunks):
            to_px(chunk, other).wait_send()

    over_px(settle)
    for halo in halos:
        halo.wait_send()
    for step in range(1, npy):
        other = lax.rem(my + step, npy)
        for index in range(len(forward)):
            piece_y(index, other, my).wait_send()
        for side in range(2):
            piece_back(side, other, my).wait_send()
    for side in range(2):
        for hop in range(npy):
            origin = lax.rem(my + hop, npy)
            own(side, origin).wait()
            over_px(lambda other: hand_on(side, origin, other).wait_send())


def fused(velocity, forcing, cross_x, cross_y, inv_x, inv_y):
    npx, npy = lax.axis_size("px"), lax.axis_size("py")
    levels, rows, cols = velocity.shape
    part = rows // npy
    half, chunks = part // 2, cols // 128
    wide = cols // chunks
    shape, narrow = velocity.shape, jnp.bfloat16
    order_x, order_y = npx * rows, npy * cols
    vmem, dma = pltpu.VMEM, pltpu.SemaphoreType.DMA
    settled = pl.pallas_call(
        functools.partial(kernel, npx, npy),
        out_shape=jax.ShapeDtypeStruct(shape, narrow),
        in_specs=[pl.BlockSpec(memory_space=pl.ANY)] * 6,
        out_specs=pl.BlockSpec(memory_space=pl.ANY),
        scratch_shapes=[
            vmem(shape, jnp.float32),
            vmem(shape, narrow),
            vmem(shape, narrow),
            vmem(shape, narrow),
            vmem((npx, rows, order_x), narrow),
            vmem((order_y, order_y), narrow),
            vmem((levels, 8, cols), jnp.float32),
            vmem((levels, 8, cols), jnp.float32),
            vmem((2, levels, rows), jnp.float32),
            vmem((2, levels, rows), jnp.float32),
            vmem((levels + 2, rows, cols), jnp.float32),
            vmem((levels + 2, rows, cols), jnp.float32),
            vmem(shape, jnp.float32),
            vmem((chunks, levels, rows, wide), narrow),
            vmem((chunks, npx, rows, wide), narrow),
            vmem((chunks + 1, npy, npx, part, wide), narrow),
            vmem((npx, part, order_y), narrow),
            vmem((2, npy, npx, half, cols), narrow),
            vmem((2, npy, npx, half, cols), narrow),
            dma((6,)),
            dma((4,)),
            dma((4,)),
            dma((chunks, npx)),
            dma((chunks, npx)),
            dma((chunks + 1, npy)),
            dma((chunks + 1, npy)),
            dma((2, npy)),
            dma((2, npy)),
            dma((2, npy, npx)),
            dma((npx,)),
            dma((2, npy)),
        ],
        compiler_params=pltpu.CompilerParams(collective_id=0, has_side_effects=True, vmem_limit_bytes=67_043_328),
        cost_estimate=pl.CostEstimate(flops=4 * order_x * order_y * rows, bytes_accessed=8 * 1024 * 1024, transcendentals=0),
    )(
        velocity,
        forcing,
        cross_x,
        cross_y,
        inv_x.reshape(npx, rows, order_x),
        inv_y.reshape(order_y, order_y),
    )
    return velocity + settled.astype(jnp.float32)


def step(velocity, forcing, cross_x, cross_y, inv_x, inv_y):
    npx, npy = lax.axis_size("px"), lax.axis_size("py")
    levels, rows, cols = velocity.shape
    aligned = rows % (32 * npy) == 0 and rows % 128 == 0 and cols % 128 == 0 and levels % 8 == 0
    if aligned and levels == npx and levels <= 128 and inv_x.shape[0] == 1:
        return fused(velocity, forcing, cross_x, cross_y, inv_x, inv_y)
    return shards(velocity, forcing, cross_x, cross_y, inv_x, inv_y)


def solution(mesh):
    return jax.shard_map(
        step,
        mesh=mesh,
        in_specs=(
            P(None, "px", "py"),
            P(None, "px", "py"),
            P(None, "px", "py"),
            P(None, "px", "py"),
            P("px", None, None),
            P("px", None, None),
        ),
        out_specs=P(None, "px", "py"),
        check_vma=False,
    )
```

```python
import functools

import jax
import jax.numpy as jnp
from jax import lax
from jax.experimental import pallas as pl
from jax.experimental.pallas import tpu as pltpu
from jax.sharding import PartitionSpec as P

time_step = 0.25


def with_halo(cells, sides, width):
    for axis, dim in sides:
        count = lax.axis_size(axis)
        head = lax.slice_in_dim(cells, 0, width, axis=dim)
        tail = lax.slice_in_dim(cells, cells.shape[dim] - width, cells.shape[dim], axis=dim)
        cells = jnp.concatenate(
            [
                lax.ppermute(tail, axis, [(i, (i + 1) % count) for i in range(count)]),
                cells,
                lax.ppermute(head, axis, [((i + 1) % count, i) for i in range(count)]),
            ],
            axis=dim,
        )
    return cells


def shards(velocity, forcing, cross_x, cross_y, inv_x, inv_y):
    padded = with_halo(velocity, (("px", 1), ("py", 2)), 1)
    x_plus = padded[:, 2:, 1:-1]
    x_minus = padded[:, :-2, 1:-1]
    y_plus = padded[:, 1:-1, 2:]
    y_minus = padded[:, 1:-1, :-2]
    z_padded = jnp.pad(velocity, ((1, 1), (0, 0), (0, 0)))
    laplace = (
        x_plus
        + x_minus
        + y_plus
        + y_minus
        - 4.0 * velocity
        + z_padded[2:]
        + z_padded[:-2]
        - 2.0 * velocity
    )
    slope_x = jnp.pad(0.5 * (x_plus - x_minus), ((1, 1), (0, 0), (0, 0)))
    slope_y = jnp.pad(0.5 * (y_plus - y_minus), ((1, 1), (0, 0), (0, 0)))
    mixed_x = 0.5 * (slope_x[2:] - slope_x[:-2])
    mixed_y = 0.5 * (slope_y[2:] - slope_y[:-2])
    total = (
        laplace
        + cross_x.astype(jnp.float32) * mixed_x
        + cross_y.astype(jnp.float32) * mixed_y
        + forcing.astype(jnp.float32)
    )
    rhs = (time_step * total).astype(jnp.bfloat16)
    section_one = jnp.einsum(
        "lab,lbk->lak",
        inv_x,
        lax.all_to_all(rhs, "px", split_axis=0, concat_axis=1, tiled=True),
        preferred_element_type=jnp.float32,
    ).astype(jnp.bfloat16)
    y_lines = lax.all_to_all(section_one, "py", split_axis=1, concat_axis=2, tiled=True)
    section_two = jnp.einsum("lxb,lab->lxa", y_lines, inv_y, preferred_element_type=jnp.float32)
    settled = lax.all_to_all(
        lax.all_to_all(section_two, "py", split_axis=2, concat_axis=1, tiled=True),
        "px",
        split_axis=1,
        concat_axis=0,
        tiled=True,
    )
    return velocity + settled


def send(src, dst, send_sem, recv_sem, target):
    return pltpu.make_async_remote_copy(
        src_ref=src,
        dst_ref=dst,
        send_sem=send_sem,
        recv_sem=recv_sem,
        device_id=target,
        device_id_type=pl.DeviceIdType.MESH,
    )


def kernel(
    npx,
    npy,
    vel_hbm,
    frc_hbm,
    cx_hbm,
    cy_hbm,
    ix_hbm,
    iy_hbm,
    out,
    vel,
    frc,
    cx,
    cy,
    ix,
    iy,
    x_low,
    x_high,
    y_send,
    y_recv,
    slope_x,
    slope_y,
    lap,
    rhs,
    lines_x,
    one,
    lines_y,
    two,
    load_sem,
    halo_send,
    halo_recv,
    rhs_send,
    rhs_recv,
    one_send,
    one_recv,
    two_send,
    out_recv,
):
    me = lax.axis_index("px")
    my = lax.axis_index("py")
    levels, rows, cols = vel.shape
    part = rows // npy
    chunks = rhs.shape[0]
    wide = cols // chunks
    pieces = [(vel_hbm, vel), (frc_hbm, frc), (cx_hbm, cx), (cy_hbm, cy), (ix_hbm, ix), (iy_hbm, iy)]
    loads = [pltpu.make_async_copy(a, b, load_sem.at[i]) for i, (a, b) in enumerate(pieces)]
    loads[0].start()

    barrier = pltpu.get_barrier_semaphore()
    for step in range(1, npx):
        pl.semaphore_signal(barrier, inc=1, device_id={"px": lax.rem(me + step, npx)}, device_id_type=pl.DeviceIdType.MESH)
    for step in range(1, npy):
        pl.semaphore_signal(barrier, inc=1, device_id={"py": lax.rem(my + step, npy)}, device_id_type=pl.DeviceIdType.MESH)

    loads[0].wait()
    for load in loads[1:]:
        load.start()
    lane = lax.broadcasted_iota(jnp.int32, (rows, 128), 1)

    def gather_face(level, faces):
        first, last = faces
        now = vel[level]
        first = jnp.where(lane == level, now[:, 0:1], first)
        last = jnp.where(lane == level, now[:, cols - 1 : cols], last)
        return first, last

    zero = jnp.zeros((rows, 128), jnp.float32)
    first, last = lax.fori_loop(0, levels, gather_face, (zero, zero))
    y_send[0] = jnp.transpose(first)[:levels]
    y_send[1] = jnp.transpose(last)[:levels]
    pl.semaphore_wait(barrier, npx + npy - 2)

    up_x, down_x = lax.rem(me + 1, npx), lax.rem(me + npx - 1, npx)
    up_y, down_y = lax.rem(my + 1, npy), lax.rem(my + npy - 1, npy)
    halos = [
        send(y_send.at[1], y_recv.at[0], halo_send.at[0], halo_recv.at[0], {"py": up_y}),
        send(y_send.at[0], y_recv.at[1], halo_send.at[1], halo_recv.at[1], {"py": down_y}),
        send(vel.at[:, pl.ds(rows - 8, 8), :], x_low, halo_send.at[2], halo_recv.at[2], {"px": up_x}),
        send(vel.at[:, pl.ds(0, 8), :], x_high, halo_send.at[3], halo_recv.at[3], {"px": down_x}),
    ]
    for halo in halos:
        halo.start()
    row_at = lax.broadcasted_iota(jnp.int32, (rows, cols), 0)
    col_at = lax.broadcasted_iota(jnp.int32, (rows, cols), 1)
    blank = jnp.zeros((rows, cols), jnp.float32)
    for edge in (0, levels + 1):
        slope_x[edge] = blank
        slope_y[edge] = blank

    def slopes(level, _):
        now = vel[level]
        x_minus = jnp.where(row_at == 0, 0.0, pltpu.roll(now, 1, 0))
        x_plus = jnp.where(row_at == rows - 1, 0.0, pltpu.roll(now, rows - 1, 0))
        y_minus = jnp.where(col_at == 0, 0.0, pltpu.roll(now, 1, 1))
        y_plus = jnp.where(col_at == cols - 1, 0.0, pltpu.roll(now, cols - 1, 1))
        slope_x[level + 1] = 0.5 * (x_plus - x_minus)
        slope_y[level + 1] = 0.5 * (y_plus - y_minus)
        lap[level] = x_plus + x_minus + y_plus + y_minus - 4.0 * now
        return 0

    lax.fori_loop(0, levels, slopes, 0)
    for load in loads[1:4]:
        load.wait()

    def inner(level, _):
        above = jnp.minimum(level + 1, levels - 1)
        below = jnp.maximum(level - 1, 0)
        z_plus = jnp.where(level < levels - 1, 1.0, 0.0) * vel[above]
        z_minus = jnp.where(level > 0, 1.0, 0.0) * vel[below]
        total = lap[level] + z_plus + z_minus - 2.0 * vel[level]
        total += cx[level].astype(jnp.float32) * (0.5 * (slope_x[level + 2] - slope_x[level]))
        total += cy[level].astype(jnp.float32) * (0.5 * (slope_y[level + 2] - slope_y[level]))
        lap[level] = total + frc[level].astype(jnp.float32)
        return 0

    lax.fori_loop(0, levels, inner, 0)
    for halo in halos:
        halo.wait_recv()

    def level_slope(face, axis, at):
        size = face.shape[axis]
        lower = jnp.where(at == 0, 0.0, pltpu.roll(face, 1, axis))
        upper = jnp.where(at == levels - 1, 0.0, pltpu.roll(face, size - 1, axis))
        return 0.25 * (upper - lower)

    spare = jnp.zeros((128 - levels, rows), jnp.float32)
    face_low = jnp.transpose(jnp.concatenate([y_recv[0], spare], axis=0))
    face_high = jnp.transpose(jnp.concatenate([y_recv[1], spare], axis=0))
    mixed_low = -level_slope(face_low, 1, lane)
    mixed_high = level_slope(face_high, 1, lane)
    level_at = lax.broadcasted_iota(jnp.int32, (levels, cols), 0)
    x_face = (x_low[:, 7, :], x_high[:, 0, :])
    x_mixed = (-level_slope(x_face[0], 0, level_at), level_slope(x_face[1], 0, level_at))
    slab_at = lax.broadcasted_iota(jnp.int32, (16, wide), 0)
    wide_at = lax.broadcasted_iota(jnp.int32, (rows, wide), 1)

    def right_side(chunk, at):
        level = lax.rem(me + 1 + at, npx)
        side = slice(chunk * wide, (chunk + 1) * wide)

        def row(faces):
            return jnp.sum(jnp.where(level_at[:, side] == level, faces, 0.0), axis=0, keepdims=True)

        for end, first in enumerate((0, rows - 16)):
            slab = slice(first, first + 16)
            face = row(x_face[end][:, side]) + cx[level, slab, side].astype(jnp.float32) * row(x_mixed[end][:, side])
            lap[level, slab, side] += jnp.where(slab_at == 15 * end, face, 0.0)
        total = lap[level, :, side]

        def column(faces):
            return jnp.sum(jnp.where(lane == level, faces, 0.0), axis=1, keepdims=True)

        for at_chunk, at_col, faces, mixed in ((0, 0, face_low, mixed_low), (chunks - 1, wide - 1, face_high, mixed_high)):
            if chunk == at_chunk:
                face = column(faces) + cy[level, :, side].astype(jnp.float32) * column(mixed)
                total += jnp.where(wide_at == at_col, face, 0.0)
        value = (time_step * total).astype(jnp.bfloat16)

        @pl.when(at < npx - 1)
        def _():
            rhs[chunk, level] = value
            to_px(chunk, level).start()

        @pl.when(at == npx - 1)
        def _():
            lines_x[chunk, me] = value

    def to_px(chunk, other):
        return send(
            rhs.at[chunk, other], lines_x.at[chunk, me], rhs_send.at[chunk, other], rhs_recv.at[chunk, me], {"px": other}
        )

    def from_px(chunk, other):
        return send(
            rhs.at[chunk, other], lines_x.at[chunk, other], rhs_send.at[chunk, other], rhs_recv.at[chunk, other], {"px": other}
        )

    def over_px(body):
        def one_step(at, _):
            body(lax.rem(me + at, npx))
            return 0

        lax.fori_loop(1, npx, one_step, 0)

    for chunk in range(chunks):
        def one_level(at, _):
            right_side(chunk, at)
            return 0

        lax.fori_loop(0, npx, one_level, 0)

    half = part // 2
    forward = [(chunk, 0, part) for chunk in range(chunks - 1)] + [(chunks - 1, 0, half), (chunks - 1, half, half)]
    order = [*range(1, npy), 0]
    turn = jnp.where(my < npy // 2, 1, npy - 1)

    def mate(step):
        return lax.rem(my + step * turn, npy)

    order_x, order_y = npx * rows, npy * cols

    def strip(at, chunk=0, width=cols):
        return pl.ds(pl.multiple_of(at * cols + chunk * wide, wide), width)

    def piece_y(index, other, source):
        chunk, first, count = forward[index]
        return send(
            one.at[index, other, :, pl.ds(0, count)],
            lines_y.at[:, pl.ds(first, count), strip(source, chunk, wide)],
            one_send.at[index, other],
            one_recv.at[index, source],
            {"py": other},
        )

    loads[4].wait()
    for index, (chunk, first, count) in enumerate(forward):
        if first == 0:
            over_px(lambda other: from_px(chunk, other).wait_recv())
        for step in order:
            other = mate(step)
            mine = ix[:, pl.ds(pl.multiple_of(other * part + first, half), count), :].reshape(npx * count, order_x)
            value = jnp.dot(mine, lines_x[chunk].reshape(order_x, wide), preferred_element_type=jnp.float32)
            value = value.astype(jnp.bfloat16).reshape(npx, count, wide)
            if step:
                one[index, other, :, 0:count] = value
                piece_y(index, other, my).start()
            else:
                lines_y[:, first : first + count, strip(my, chunk, wide)] = value

    def cut(side, origin):
        return pl.ds(pl.multiple_of(origin * part + side * half, half), half)

    def to_cells(side, other_y, other_x):
        return send(
            two.at[side, other_y, other_x],
            out.at[me, cut(side, my), :],
            two_send.at[side, other_y, other_x],
            out_recv.at[me],
            {"px": other_x, "py": other_y},
        )

    def own(side):
        return pltpu.make_async_copy(two.at[side, my, me], out.at[me, cut(side, my), :], out_recv.at[me])

    loads[5].wait()
    for side in range(2):
        for index, (chunk, first, count) in enumerate(forward):
            if first == side * half:
                for step in range(1, npy):
                    source = lax.rem(my + step, npy)
                    piece_y(index, source, source).wait_recv()
        held = lines_y[:, side * half : (side + 1) * half, :].reshape(npx * half, order_y)
        for step in order:
            other = mate(step)
            value = lax.dot_general(held, iy[strip(other), :], (((1,), (1,)), ((), ())), preferred_element_type=jnp.float32)
            two[side, other] = value.astype(jnp.bfloat16).reshape(npx, half, cols)
            over_px(lambda other_x: to_cells(side, other, other_x).start())
            if step:
                to_cells(side, other, me).start()
            else:
                own(side).start()

    def settle(other):
        send(out.at[other], out.at[other], rhs_send.at[0, other], out_recv.at[other], {"px": other}).wait_recv()
        for chunk in range(chunks):
            to_px(chunk, other).wait_send()

    over_px(settle)
    pltpu.make_async_copy(out.at[me], out.at[me], out_recv.at[me]).wait()
    for halo in halos:
        halo.wait_send()
    for step in range(1, npy):
        other = lax.rem(my + step, npy)
        for index in range(len(forward)):
            piece_y(index, other, my).wait_send()
    for side in range(2):
        for step in range(npy):
            other = lax.rem(my + step, npy)
            over_px(lambda other_x: to_cells(side, other, other_x).wait_send())
            if step:
                to_cells(side, other, me).wait_send()


def fused(velocity, forcing, cross_x, cross_y, inv_x, inv_y):
    npx, npy = lax.axis_size("px"), lax.axis_size("py")
    levels, rows, cols = velocity.shape
    part = rows // npy
    half, chunks = part // 2, cols // 128
    wide = cols // chunks
    shape, narrow = velocity.shape, jnp.bfloat16
    order_x, order_y = npx * rows, npy * cols
    vmem, dma = pltpu.VMEM, pltpu.SemaphoreType.DMA
    settled = pl.pallas_call(
        functools.partial(kernel, npx, npy),
        out_shape=jax.ShapeDtypeStruct(shape, narrow),
        in_specs=[pl.BlockSpec(memory_space=pl.ANY)] * 6,
        out_specs=pl.BlockSpec(memory_space=pl.ANY),
        scratch_shapes=[
            vmem(shape, jnp.float32),
            vmem(shape, narrow),
            vmem(shape, narrow),
            vmem(shape, narrow),
            vmem((npx, rows, order_x), narrow),
            vmem((order_y, order_y), narrow),
            vmem((levels, 8, cols), jnp.float32),
            vmem((levels, 8, cols), jnp.float32),
            vmem((2, levels, rows), jnp.float32),
            vmem((2, levels, rows), jnp.float32),
            vmem((levels + 2, rows, cols), jnp.float32),
            vmem((levels + 2, rows, cols), jnp.float32),
            vmem(shape, jnp.float32),
            vmem((chunks, levels, rows, wide), narrow),
            vmem((chunks, npx, rows, wide), narrow),
            vmem((chunks + 1, npy, npx, part, wide), narrow),
            vmem((npx, part, order_y), narrow),
            vmem((2, npy, npx, half, cols), narrow),
            dma((6,)),
            dma((4,)),
            dma((4,)),
            dma((chunks, npx)),
            dma((chunks, npx)),
            dma((chunks + 1, npy)),
            dma((chunks + 1, npy)),
            dma((2, npy, npx)),
            dma((npx,)),
        ],
        compiler_params=pltpu.CompilerParams(collective_id=0, has_side_effects=True, vmem_limit_bytes=67_043_328),
        cost_estimate=pl.CostEstimate(flops=4 * order_x * order_y * rows, bytes_accessed=8 * 1024 * 1024, transcendentals=0),
    )(
        velocity,
        forcing,
        cross_x,
        cross_y,
        inv_x.reshape(npx, rows, order_x),
        inv_y.reshape(order_y, order_y),
    )
    return velocity + settled.astype(jnp.float32)


def step(velocity, forcing, cross_x, cross_y, inv_x, inv_y):
    npx, npy = lax.axis_size("px"), lax.axis_size("py")
    levels, rows, cols = velocity.shape
    aligned = rows % (32 * npy) == 0 and rows % 128 == 0 and cols % 128 == 0 and levels % 8 == 0
    if aligned and levels == npx and levels <= 128 and inv_x.shape[0] == 1:
        return fused(velocity, forcing, cross_x, cross_y, inv_x, inv_y)
    return shards(velocity, forcing, cross_x, cross_y, inv_x, inv_y)


def solution(mesh):
    return jax.shard_map(
        step,
        mesh=mesh,
        in_specs=(
            P(None, "px", "py"),
            P(None, "px", "py"),
            P(None, "px", "py"),
            P(None, "px", "py"),
            P("px", None, None),
            P("px", None, None),
        ),
        out_specs=P(None, "px", "py"),
        check_vma=False,
    )
```

```python
import functools

import jax
import jax.numpy as jnp
from jax import lax
from jax.experimental import pallas as pl
from jax.experimental.pallas import tpu as pltpu
from jax.sharding import PartitionSpec as P

time_step = 0.25


def with_halo(cells, sides, width):
    for axis, dim in sides:
        count = lax.axis_size(axis)
        head = lax.slice_in_dim(cells, 0, width, axis=dim)
        tail = lax.slice_in_dim(cells, cells.shape[dim] - width, cells.shape[dim], axis=dim)
        cells = jnp.concatenate(
            [
                lax.ppermute(tail, axis, [(i, (i + 1) % count) for i in range(count)]),
                cells,
                lax.ppermute(head, axis, [((i + 1) % count, i) for i in range(count)]),
            ],
            axis=dim,
        )
    return cells


def shards(velocity, forcing, cross_x, cross_y, inv_x, inv_y):
    padded = with_halo(velocity, (("px", 1), ("py", 2)), 1)
    x_plus = padded[:, 2:, 1:-1]
    x_minus = padded[:, :-2, 1:-1]
    y_plus = padded[:, 1:-1, 2:]
    y_minus = padded[:, 1:-1, :-2]
    z_padded = jnp.pad(velocity, ((1, 1), (0, 0), (0, 0)))
    laplace = (
        x_plus
        + x_minus
        + y_plus
        + y_minus
        - 4.0 * velocity
        + z_padded[2:]
        + z_padded[:-2]
        - 2.0 * velocity
    )
    slope_x = jnp.pad(0.5 * (x_plus - x_minus), ((1, 1), (0, 0), (0, 0)))
    slope_y = jnp.pad(0.5 * (y_plus - y_minus), ((1, 1), (0, 0), (0, 0)))
    mixed_x = 0.5 * (slope_x[2:] - slope_x[:-2])
    mixed_y = 0.5 * (slope_y[2:] - slope_y[:-2])
    total = (
        laplace
        + cross_x.astype(jnp.float32) * mixed_x
        + cross_y.astype(jnp.float32) * mixed_y
        + forcing.astype(jnp.float32)
    )
    rhs = (time_step * total).astype(jnp.bfloat16)
    section_one = jnp.einsum(
        "lab,lbk->lak",
        inv_x,
        lax.all_to_all(rhs, "px", split_axis=0, concat_axis=1, tiled=True),
        preferred_element_type=jnp.float32,
    ).astype(jnp.bfloat16)
    y_lines = lax.all_to_all(section_one, "py", split_axis=1, concat_axis=2, tiled=True)
    section_two = jnp.einsum("lxb,lab->lxa", y_lines, inv_y, preferred_element_type=jnp.float32)
    settled = lax.all_to_all(
        lax.all_to_all(section_two, "py", split_axis=2, concat_axis=1, tiled=True),
        "px",
        split_axis=1,
        concat_axis=0,
        tiled=True,
    )
    return velocity + settled


def send(src, dst, send_sem, recv_sem, target):
    return pltpu.make_async_remote_copy(
        src_ref=src,
        dst_ref=dst,
        send_sem=send_sem,
        recv_sem=recv_sem,
        device_id=target,
        device_id_type=pl.DeviceIdType.MESH,
    )


def kernel(
    npx,
    npy,
    vel_hbm,
    frc_hbm,
    cx_hbm,
    cy_hbm,
    ix_hbm,
    iy_hbm,
    out,
    vel,
    frc,
    cx,
    cy,
    ix,
    iy,
    x_low,
    x_high,
    y_send,
    y_recv,
    slope_x,
    slope_y,
    lap,
    rhs,
    lines_x,
    one,
    lines_y,
    two,
    load_sem,
    halo_send,
    halo_recv,
    rhs_send,
    rhs_recv,
    one_send,
    one_recv,
    two_send,
    out_recv,
):
    me = lax.axis_index("px")
    my = lax.axis_index("py")
    levels, rows, cols = vel.shape
    part = rows // npy
    chunks = rhs.shape[0]
    wide = cols // chunks
    pieces = [(vel_hbm, vel), (frc_hbm, frc), (cx_hbm, cx), (cy_hbm, cy), (ix_hbm, ix), (iy_hbm, iy)]
    loads = [pltpu.make_async_copy(a, b, load_sem.at[i]) for i, (a, b) in enumerate(pieces)]
    loads[0].start()

    barrier = pltpu.get_barrier_semaphore()
    for step in range(1, npx):
        pl.semaphore_signal(barrier, inc=1, device_id={"px": lax.rem(me + step, npx)}, device_id_type=pl.DeviceIdType.MESH)
    for step in range(1, npy):
        pl.semaphore_signal(barrier, inc=1, device_id={"py": lax.rem(my + step, npy)}, device_id_type=pl.DeviceIdType.MESH)

    loads[0].wait()
    for load in loads[1:]:
        load.start()
    lane = lax.broadcasted_iota(jnp.int32, (rows, 128), 1)

    def gather_face(level, faces):
        first, last = faces
        now = vel[level]
        first = jnp.where(lane == level, now[:, 0:1], first)
        last = jnp.where(lane == level, now[:, cols - 1 : cols], last)
        return first, last

    zero = jnp.zeros((rows, 128), jnp.float32)
    first, last = lax.fori_loop(0, levels, gather_face, (zero, zero))
    y_send[0] = jnp.transpose(first)[:levels]
    y_send[1] = jnp.transpose(last)[:levels]
    pl.semaphore_wait(barrier, npx + npy - 2)

    up_x, down_x = lax.rem(me + 1, npx), lax.rem(me + npx - 1, npx)
    up_y, down_y = lax.rem(my + 1, npy), lax.rem(my + npy - 1, npy)
    halos = [
        send(y_send.at[1], y_recv.at[0], halo_send.at[0], halo_recv.at[0], {"py": up_y}),
        send(y_send.at[0], y_recv.at[1], halo_send.at[1], halo_recv.at[1], {"py": down_y}),
        send(vel.at[:, pl.ds(rows - 8, 8), :], x_low, halo_send.at[2], halo_recv.at[2], {"px": up_x}),
        send(vel.at[:, pl.ds(0, 8), :], x_high, halo_send.at[3], halo_recv.at[3], {"px": down_x}),
    ]
    for halo in halos:
        halo.start()
    row_at = lax.broadcasted_iota(jnp.int32, (rows, cols), 0)
    col_at = lax.broadcasted_iota(jnp.int32, (rows, cols), 1)
    blank = jnp.zeros((rows, cols), jnp.float32)
    for edge in (0, levels + 1):
        slope_x[edge] = blank
        slope_y[edge] = blank

    def slopes(level, _):
        now = vel[level]
        x_minus = jnp.where(row_at == 0, 0.0, pltpu.roll(now, 1, 0))
        x_plus = jnp.where(row_at == rows - 1, 0.0, pltpu.roll(now, rows - 1, 0))
        y_minus = jnp.where(col_at == 0, 0.0, pltpu.roll(now, 1, 1))
        y_plus = jnp.where(col_at == cols - 1, 0.0, pltpu.roll(now, cols - 1, 1))
        slope_x[level + 1] = 0.5 * (x_plus - x_minus)
        slope_y[level + 1] = 0.5 * (y_plus - y_minus)
        lap[level] = x_plus + x_minus + y_plus + y_minus - 4.0 * now
        return 0

    lax.fori_loop(0, levels, slopes, 0)
    for load in loads[1:4]:
        load.wait()

    def inner(level, _):
        above = jnp.minimum(level + 1, levels - 1)
        below = jnp.maximum(level - 1, 0)
        z_plus = jnp.where(level < levels - 1, 1.0, 0.0) * vel[above]
        z_minus = jnp.where(level > 0, 1.0, 0.0) * vel[below]
        total = lap[level] + z_plus + z_minus - 2.0 * vel[level]
        total += cx[level].astype(jnp.float32) * (0.5 * (slope_x[level + 2] - slope_x[level]))
        total += cy[level].astype(jnp.float32) * (0.5 * (slope_y[level + 2] - slope_y[level]))
        lap[level] = total + frc[level].astype(jnp.float32)
        return 0

    lax.fori_loop(0, levels, inner, 0)
    for halo in halos:
        halo.wait_recv()

    def level_slope(face, axis, at):
        size = face.shape[axis]
        lower = jnp.where(at == 0, 0.0, pltpu.roll(face, 1, axis))
        upper = jnp.where(at == levels - 1, 0.0, pltpu.roll(face, size - 1, axis))
        return 0.25 * (upper - lower)

    spare = jnp.zeros((128 - levels, rows), jnp.float32)
    face_low = jnp.transpose(jnp.concatenate([y_recv[0], spare], axis=0))
    face_high = jnp.transpose(jnp.concatenate([y_recv[1], spare], axis=0))
    mixed_low = -level_slope(face_low, 1, lane)
    mixed_high = level_slope(face_high, 1, lane)
    level_at = lax.broadcasted_iota(jnp.int32, (levels, cols), 0)
    x_face = (x_low[:, 7, :], x_high[:, 0, :])
    x_mixed = (-level_slope(x_face[0], 0, level_at), level_slope(x_face[1], 0, level_at))
    slab_at = lax.broadcasted_iota(jnp.int32, (16, wide), 0)
    wide_at = lax.broadcasted_iota(jnp.int32, (rows, wide), 1)

    def right_side(chunk, at):
        level = lax.rem(me + 1 + at, npx)
        side = slice(chunk * wide, (chunk + 1) * wide)

        def row(faces):
            return jnp.sum(jnp.where(level_at[:, side] == level, faces, 0.0), axis=0, keepdims=True)

        for end, first in enumerate((0, rows - 16)):
            slab = slice(first, first + 16)
            face = row(x_face[end][:, side]) + cx[level, slab, side].astype(jnp.float32) * row(x_mixed[end][:, side])
            lap[level, slab, side] += jnp.where(slab_at == 15 * end, face, 0.0)
        total = lap[level, :, side]

        def column(faces):
            return jnp.sum(jnp.where(lane == level, faces, 0.0), axis=1, keepdims=True)

        for at_chunk, at_col, faces, mixed in ((0, 0, face_low, mixed_low), (chunks - 1, wide - 1, face_high, mixed_high)):
            if chunk == at_chunk:
                face = column(faces) + cy[level, :, side].astype(jnp.float32) * column(mixed)
                total += jnp.where(wide_at == at_col, face, 0.0)
        value = (time_step * total).astype(jnp.bfloat16)

        @pl.when(at < npx - 1)
        def _():
            rhs[chunk, level] = value
            to_px(chunk, level).start()

        @pl.when(at == npx - 1)
        def _():
            lines_x[chunk, me] = value

    def to_px(chunk, other):
        return send(
            rhs.at[chunk, other], lines_x.at[chunk, me], rhs_send.at[chunk, other], rhs_recv.at[chunk, me], {"px": other}
        )

    def from_px(chunk, other):
        return send(
            rhs.at[chunk, other], lines_x.at[chunk, other], rhs_send.at[chunk, other], rhs_recv.at[chunk, other], {"px": other}
        )

    def over_px(body):
        def one_step(at, _):
            body(lax.rem(me + at, npx))
            return 0

        lax.fori_loop(1, npx, one_step, 0)

    for chunk in range(chunks):
        def one_level(at, _):
            right_side(chunk, at)
            return 0

        lax.fori_loop(0, npx, one_level, 0)

    half = part // 2
    forward = [(chunk, 0, part) for chunk in range(chunks - 1)] + [(chunks - 1, 0, half), (chunks - 1, half, half)]
    order = [*range(1, npy), 0]
    turn = jnp.where(my < npy // 2, 1, npy - 1)

    def mate(step):
        return lax.rem(my + step * turn, npy)

    order_x, order_y = npx * rows, npy * cols

    def strip(at, chunk=0, width=cols):
        return pl.ds(pl.multiple_of(at * cols + chunk * wide, wide), width)

    def piece_y(index, other, source):
        chunk, first, count = forward[index]
        return send(
            one.at[index, other, :, pl.ds(0, count)],
            lines_y.at[:, pl.ds(first, count), strip(source, chunk, wide)],
            one_send.at[index, other],
            one_recv.at[index, source],
            {"py": other},
        )

    loads[4].wait()
    for index, (chunk, first, count) in enumerate(forward):
        if first == 0:
            over_px(lambda other: from_px(chunk, other).wait_recv())
        for step in order:
            other = mate(step)
            mine = ix[:, pl.ds(pl.multiple_of(other * part + first, half), count), :].reshape(npx * count, order_x)
            value = jnp.dot(mine, lines_x[chunk].reshape(order_x, wide), preferred_element_type=jnp.float32)
            value = value.astype(jnp.bfloat16).reshape(npx, count, wide)
            if step:
                one[index, other, :, 0:count] = value
                piece_y(index, other, my).start()
            else:
                lines_y[:, first : first + count, strip(my, chunk, wide)] = value

    def cut(side, origin):
        return pl.ds(pl.multiple_of(origin * part + side * half, half), half)

    def to_cells(side, other_y, other_x):
        return send(
            two.at[side, other_y, other_x],
            out.at[me, cut(side, my), :],
            two_send.at[side, other_y, other_x],
            out_recv.at[me],
            {"px": other_x, "py": other_y},
        )

    def own(side):
        return pltpu.make_async_copy(two.at[side, my, me], out.at[me, cut(side, my), :], out_recv.at[me])

    loads[5].wait()
    for side in range(2):
        for index, (chunk, first, count) in enumerate(forward):
            if first == side * half:
                for step in range(1, npy):
                    source = lax.rem(my + step, npy)
                    piece_y(index, source, source).wait_recv()
        held = lines_y[:, side * half : (side + 1) * half, :].reshape(npx * half, order_y)
        for step in order:
            other = mate(step)
            value = lax.dot_general(held, iy[strip(other), :], (((1,), (1,)), ((), ())), preferred_element_type=jnp.float32)
            two[side, other] = value.astype(jnp.bfloat16).reshape(npx, half, cols)
            over_px(lambda other_x: to_cells(side, other, other_x).start())
            if step:
                to_cells(side, other, me).start()
            else:
                own(side).start()

    def settle(other):
        send(out.at[other], out.at[other], rhs_send.at[0, other], out_recv.at[other], {"px": other}).wait_recv()
        for chunk in range(chunks):
            to_px(chunk, other).wait_send()

    over_px(settle)
    pltpu.make_async_copy(out.at[me], out.at[me], out_recv.at[me]).wait()
    for halo in halos:
        halo.wait_send()
    for step in range(1, npy):
        other = lax.rem(my + step, npy)
        for index in range(len(forward)):
            piece_y(index, other, my).wait_send()
    for side in range(2):
        for step in range(npy):
            other = lax.rem(my + step, npy)
            over_px(lambda other_x: to_cells(side, other, other_x).wait_send())
            if step:
                to_cells(side, other, me).wait_send()


def fused(velocity, forcing, cross_x, cross_y, inv_x, inv_y):
    npx, npy = lax.axis_size("px"), lax.axis_size("py")
    levels, rows, cols = velocity.shape
    part = rows // npy
    half, chunks = part // 2, cols // 128
    wide = cols // chunks
    shape, narrow = velocity.shape, jnp.bfloat16
    order_x, order_y = npx * rows, npy * cols
    vmem, dma = pltpu.VMEM, pltpu.SemaphoreType.DMA
    settled = pl.pallas_call(
        functools.partial(kernel, npx, npy),
        out_shape=jax.ShapeDtypeStruct(shape, narrow),
        in_specs=[pl.BlockSpec(memory_space=pl.ANY)] * 6,
        out_specs=pl.BlockSpec(memory_space=pl.ANY),
        scratch_shapes=[
            vmem(shape, jnp.float32),
            vmem(shape, narrow),
            vmem(shape, narrow),
            vmem(shape, narrow),
            vmem((npx, rows, order_x), narrow),
            vmem((order_y, order_y), narrow),
            vmem((levels, 8, cols), jnp.float32),
            vmem((levels, 8, cols), jnp.float32),
            vmem((2, levels, rows), jnp.float32),
            vmem((2, levels, rows), jnp.float32),
            vmem((levels + 2, rows, cols), jnp.float32),
            vmem((levels + 2, rows, cols), jnp.float32),
            vmem(shape, jnp.float32),
            vmem((chunks, levels, rows, wide), narrow),
            vmem((chunks, npx, rows, wide), narrow),
            vmem((chunks + 1, npy, npx, part, wide), narrow),
            vmem((npx, part, order_y), narrow),
            vmem((2, npy, npx, half, cols), narrow),
            dma((6,)),
            dma((4,)),
            dma((4,)),
            dma((chunks, npx)),
            dma((chunks, npx)),
            dma((chunks + 1, npy)),
            dma((chunks + 1, npy)),
            dma((2, npy, npx)),
            dma((npx,)),
        ],
        compiler_params=pltpu.CompilerParams(collective_id=0, has_side_effects=True, vmem_limit_bytes=56_000_000),
        cost_estimate=pl.CostEstimate(flops=4 * order_x * order_y * rows, bytes_accessed=8 * 1024 * 1024, transcendentals=0),
    )(
        velocity,
        forcing,
        cross_x,
        cross_y,
        inv_x.reshape(npx, rows, order_x),
        inv_y.reshape(order_y, order_y),
    )
    return velocity + settled.astype(jnp.float32)


def step(velocity, forcing, cross_x, cross_y, inv_x, inv_y):
    npx, npy = lax.axis_size("px"), lax.axis_size("py")
    levels, rows, cols = velocity.shape
    aligned = rows % (32 * npy) == 0 and rows % 128 == 0 and cols % 128 == 0 and levels % 8 == 0
    if aligned and levels == npx and levels <= 128 and inv_x.shape[0] == 1:
        return fused(velocity, forcing, cross_x, cross_y, inv_x, inv_y)
    return shards(velocity, forcing, cross_x, cross_y, inv_x, inv_y)


def solution(mesh):
    return jax.shard_map(
        step,
        mesh=mesh,
        in_specs=(
            P(None, "px", "py"),
            P(None, "px", "py"),
            P(None, "px", "py"),
            P(None, "px", "py"),
            P("px", None, None),
            P("px", None, None),
        ),
        out_specs=P(None, "px", "py"),
        check_vma=False,
    )
```

```python
import functools

import jax
import jax.numpy as jnp
from jax import lax
from jax.experimental import pallas as pl
from jax.experimental.pallas import tpu as pltpu
from jax.sharding import PartitionSpec as P

time_step = 0.25


def with_halo(cells, sides, width):
    for axis, dim in sides:
        count = lax.axis_size(axis)
        head = lax.slice_in_dim(cells, 0, width, axis=dim)
        tail = lax.slice_in_dim(cells, cells.shape[dim] - width, cells.shape[dim], axis=dim)
        cells = jnp.concatenate(
            [
                lax.ppermute(tail, axis, [(i, (i + 1) % count) for i in range(count)]),
                cells,
                lax.ppermute(head, axis, [((i + 1) % count, i) for i in range(count)]),
            ],
            axis=dim,
        )
    return cells


def shards(velocity, forcing, cross_x, cross_y, inv_x, inv_y):
    padded = with_halo(velocity, (("px", 1), ("py", 2)), 1)
    x_plus = padded[:, 2:, 1:-1]
    x_minus = padded[:, :-2, 1:-1]
    y_plus = padded[:, 1:-1, 2:]
    y_minus = padded[:, 1:-1, :-2]
    z_padded = jnp.pad(velocity, ((1, 1), (0, 0), (0, 0)))
    laplace = (
        x_plus
        + x_minus
        + y_plus
        + y_minus
        - 4.0 * velocity
        + z_padded[2:]
        + z_padded[:-2]
        - 2.0 * velocity
    )
    slope_x = jnp.pad(0.5 * (x_plus - x_minus), ((1, 1), (0, 0), (0, 0)))
    slope_y = jnp.pad(0.5 * (y_plus - y_minus), ((1, 1), (0, 0), (0, 0)))
    mixed_x = 0.5 * (slope_x[2:] - slope_x[:-2])
    mixed_y = 0.5 * (slope_y[2:] - slope_y[:-2])
    total = (
        laplace
        + cross_x.astype(jnp.float32) * mixed_x
        + cross_y.astype(jnp.float32) * mixed_y
        + forcing.astype(jnp.float32)
    )
    rhs = (time_step * total).astype(jnp.bfloat16)
    section_one = jnp.einsum(
        "lab,lbk->lak",
        inv_x,
        lax.all_to_all(rhs, "px", split_axis=0, concat_axis=1, tiled=True),
        preferred_element_type=jnp.float32,
    ).astype(jnp.bfloat16)
    y_lines = lax.all_to_all(section_one, "py", split_axis=1, concat_axis=2, tiled=True)
    section_two = jnp.einsum("lxb,lab->lxa", y_lines, inv_y, preferred_element_type=jnp.float32)
    settled = lax.all_to_all(
        lax.all_to_all(section_two, "py", split_axis=2, concat_axis=1, tiled=True),
        "px",
        split_axis=1,
        concat_axis=0,
        tiled=True,
    )
    return velocity + settled


def send(src, dst, send_sem, recv_sem, target):
    return pltpu.make_async_remote_copy(
        src_ref=src,
        dst_ref=dst,
        send_sem=send_sem,
        recv_sem=recv_sem,
        device_id=target,
        device_id_type=pl.DeviceIdType.MESH,
    )


def kernel(
    npx,
    npy,
    vel_hbm,
    frc_hbm,
    cx_hbm,
    cy_hbm,
    ix_hbm,
    iy_hbm,
    out,
    vel,
    frc,
    cx,
    cy,
    ix,
    iy,
    x_low,
    x_high,
    y_send,
    y_recv,
    slope_x,
    slope_y,
    lap,
    rhs,
    lines_x,
    one,
    lines_y,
    two,
    load_sem,
    halo_send,
    halo_recv,
    rhs_send,
    rhs_recv,
    one_send,
    one_recv,
    two_send,
    out_recv,
):
    me = lax.axis_index("px")
    my = lax.axis_index("py")
    levels, rows, cols = vel.shape
    part = rows // npy
    chunks = rhs.shape[0]
    wide = cols // chunks
    pieces = [(vel_hbm, vel), (frc_hbm, frc), (cx_hbm, cx), (cy_hbm, cy), (ix_hbm, ix), (iy_hbm, iy)]
    loads = [pltpu.make_async_copy(a, b, load_sem.at[i]) for i, (a, b) in enumerate(pieces)]
    loads[0].start()

    barrier = pltpu.get_barrier_semaphore()
    for step in range(1, npx):
        pl.semaphore_signal(barrier, inc=1, device_id={"px": lax.rem(me + step, npx)}, device_id_type=pl.DeviceIdType.MESH)
    for step in range(1, npy):
        pl.semaphore_signal(barrier, inc=1, device_id={"py": lax.rem(my + step, npy)}, device_id_type=pl.DeviceIdType.MESH)

    loads[0].wait()
    for load in loads[1:]:
        load.start()
    lane = lax.broadcasted_iota(jnp.int32, (rows, 128), 1)

    def gather_face(level, faces):
        first, last = faces
        now = vel[level]
        first = jnp.where(lane == level, now[:, 0:1], first)
        last = jnp.where(lane == level, now[:, cols - 1 : cols], last)
        return first, last

    zero = jnp.zeros((rows, 128), jnp.float32)
    first, last = lax.fori_loop(0, levels, gather_face, (zero, zero))
    y_send[0] = jnp.transpose(first)[:levels]
    y_send[1] = jnp.transpose(last)[:levels]
    pl.semaphore_wait(barrier, npx + npy - 2)

    up_x, down_x = lax.rem(me + 1, npx), lax.rem(me + npx - 1, npx)
    up_y, down_y = lax.rem(my + 1, npy), lax.rem(my + npy - 1, npy)
    halos = [
        send(y_send.at[1], y_recv.at[0], halo_send.at[0], halo_recv.at[0], {"py": up_y}),
        send(y_send.at[0], y_recv.at[1], halo_send.at[1], halo_recv.at[1], {"py": down_y}),
        send(vel.at[:, pl.ds(rows - 8, 8), :], x_low, halo_send.at[2], halo_recv.at[2], {"px": up_x}),
        send(vel.at[:, pl.ds(0, 8), :], x_high, halo_send.at[3], halo_recv.at[3], {"px": down_x}),
    ]
    for halo in halos:
        halo.start()
    row_at = lax.broadcasted_iota(jnp.int32, (rows, cols), 0)
    col_at = lax.broadcasted_iota(jnp.int32, (rows, cols), 1)
    blank = jnp.zeros((rows, cols), jnp.float32)
    for edge in (0, levels + 1):
        slope_x[edge] = blank
        slope_y[edge] = blank

    def slopes(level, _):
        now = vel[level]
        x_minus = jnp.where(row_at == 0, 0.0, pltpu.roll(now, 1, 0))
        x_plus = jnp.where(row_at == rows - 1, 0.0, pltpu.roll(now, rows - 1, 0))
        y_minus = jnp.where(col_at == 0, 0.0, pltpu.roll(now, 1, 1))
        y_plus = jnp.where(col_at == cols - 1, 0.0, pltpu.roll(now, cols - 1, 1))
        slope_x[level + 1] = 0.5 * (x_plus - x_minus)
        slope_y[level + 1] = 0.5 * (y_plus - y_minus)
        lap[level] = x_plus + x_minus + y_plus + y_minus - 4.0 * now
        return 0

    lax.fori_loop(0, levels, slopes, 0)
    for load in loads[1:4]:
        load.wait()

    def inner(level, _):
        above = jnp.minimum(level + 1, levels - 1)
        below = jnp.maximum(level - 1, 0)
        z_plus = jnp.where(level < levels - 1, 1.0, 0.0) * vel[above]
        z_minus = jnp.where(level > 0, 1.0, 0.0) * vel[below]
        total = lap[level] + z_plus + z_minus - 2.0 * vel[level]
        total += cx[level].astype(jnp.float32) * (0.5 * (slope_x[level + 2] - slope_x[level]))
        total += cy[level].astype(jnp.float32) * (0.5 * (slope_y[level + 2] - slope_y[level]))
        lap[level] = total + frc[level].astype(jnp.float32)
        return 0

    lax.fori_loop(0, levels, inner, 0)
    for halo in halos:
        halo.wait_recv()

    def level_slope(face, axis, at):
        size = face.shape[axis]
        lower = jnp.where(at == 0, 0.0, pltpu.roll(face, 1, axis))
        upper = jnp.where(at == levels - 1, 0.0, pltpu.roll(face, size - 1, axis))
        return 0.25 * (upper - lower)

    spare = jnp.zeros((128 - levels, rows), jnp.float32)
    face_low = jnp.transpose(jnp.concatenate([y_recv[0], spare], axis=0))
    face_high = jnp.transpose(jnp.concatenate([y_recv[1], spare], axis=0))
    mixed_low = -level_slope(face_low, 1, lane)
    mixed_high = level_slope(face_high, 1, lane)
    level_at = lax.broadcasted_iota(jnp.int32, (levels, cols), 0)
    x_face = (x_low[:, 7, :], x_high[:, 0, :])
    x_mixed = (-level_slope(x_face[0], 0, level_at), level_slope(x_face[1], 0, level_at))
    slab_at = lax.broadcasted_iota(jnp.int32, (16, wide), 0)
    wide_at = lax.broadcasted_iota(jnp.int32, (rows, wide), 1)

    def right_side(chunk, at):
        ahead = jnp.where(at == npx - 1, 0, lax.rem(at + npx // 4, npx - 1) + 1)
        level = lax.rem(me + ahead, npx)
        side = slice(chunk * wide, (chunk + 1) * wide)

        def row(faces):
            return jnp.sum(jnp.where(level_at[:, side] == level, faces, 0.0), axis=0, keepdims=True)

        for end, first in enumerate((0, rows - 16)):
            slab = slice(first, first + 16)
            face = row(x_face[end][:, side]) + cx[level, slab, side].astype(jnp.float32) * row(x_mixed[end][:, side])
            lap[level, slab, side] += jnp.where(slab_at == 15 * end, face, 0.0)
        total = lap[level, :, side]

        def column(faces):
            return jnp.sum(jnp.where(lane == level, faces, 0.0), axis=1, keepdims=True)

        for at_chunk, at_col, faces, mixed in ((0, 0, face_low, mixed_low), (chunks - 1, wide - 1, face_high, mixed_high)):
            if chunk == at_chunk:
                face = column(faces) + cy[level, :, side].astype(jnp.float32) * column(mixed)
                total += jnp.where(wide_at == at_col, face, 0.0)
        value = (time_step * total).astype(jnp.bfloat16)

        @pl.when(at < npx - 1)
        def _():
            rhs[chunk, level] = value
            to_px(chunk, level).start()

        @pl.when(at == npx - 1)
        def _():
            lines_x[chunk, me] = value

    def to_px(chunk, other):
        return send(
            rhs.at[chunk, other], lines_x.at[chunk, me], rhs_send.at[chunk, other], rhs_recv.at[chunk, me], {"px": other}
        )

    def from_px(chunk, other):
        return send(
            rhs.at[chunk, other], lines_x.at[chunk, other], rhs_send.at[chunk, other], rhs_recv.at[chunk, other], {"px": other}
        )

    def over_px(body):
        def one_step(at, _):
            body(lax.rem(me + at, npx))
            return 0

        lax.fori_loop(1, npx, one_step, 0)

    for chunk in range(chunks):
        def one_level(at, _):
            right_side(chunk, at)
            return 0

        lax.fori_loop(0, npx, one_level, 0)

    half = part // 2
    forward = [(chunk, 0, part) for chunk in range(chunks - 1)] + [(chunks - 1, 0, half), (chunks - 1, half, half)]
    order = [*range(1, npy), 0]
    turn = jnp.where(my < npy // 2, 1, npy - 1)

    def mate(step):
        return lax.rem(my + step * turn, npy)

    order_x, order_y = npx * rows, npy * cols

    def strip(at, chunk=0, width=cols):
        return pl.ds(pl.multiple_of(at * cols + chunk * wide, wide), width)

    def piece_y(index, other, source):
        chunk, first, count = forward[index]
        return send(
            one.at[index, other, :, pl.ds(0, count)],
            lines_y.at[:, pl.ds(first, count), strip(source, chunk, wide)],
            one_send.at[index, other],
            one_recv.at[index, source],
            {"py": other},
        )

    loads[4].wait()
    for index, (chunk, first, count) in enumerate(forward):
        if first == 0:
            over_px(lambda other: from_px(chunk, other).wait_recv())
        for step in order:
            other = mate(step)
            mine = ix[:, pl.ds(pl.multiple_of(other * part + first, half), count), :].reshape(npx * count, order_x)
            value = jnp.dot(mine, lines_x[chunk].reshape(order_x, wide), preferred_element_type=jnp.float32)
            value = value.astype(jnp.bfloat16).reshape(npx, count, wide)
            if step:
                one[index, other, :, 0:count] = value
                piece_y(index, other, my).start()
            else:
                lines_y[:, first : first + count, strip(my, chunk, wide)] = value

    def cut(side, origin):
        return pl.ds(pl.multiple_of(origin * part + side * half, half), half)

    def to_cells(side, other_y, other_x):
        return send(
            two.at[side, other_y, other_x],
            out.at[me, cut(side, my), :],
            two_send.at[side, other_y, other_x],
            out_recv.at[me],
            {"px": other_x, "py": other_y},
        )

    def own(side):
        return pltpu.make_async_copy(two.at[side, my, me], out.at[me, cut(side, my), :], out_recv.at[me])

    loads[5].wait()
    for side in range(2):
        for index, (chunk, first, count) in enumerate(forward):
            if first == side * half:
                for step in range(1, npy):
                    source = lax.rem(my + step, npy)
                    piece_y(index, source, source).wait_recv()
        held = lines_y[:, side * half : (side + 1) * half, :].reshape(npx * half, order_y)
        for step in order:
            other = mate(step)
            value = lax.dot_general(held, iy[strip(other), :], (((1,), (1,)), ((), ())), preferred_element_type=jnp.float32)
            two[side, other] = value.astype(jnp.bfloat16).reshape(npx, half, cols)
            over_px(lambda other_x: to_cells(side, other, other_x).start())
            if step:
                to_cells(side, other, me).start()
            else:
                own(side).start()

    def settle(other):
        send(out.at[other], out.at[other], rhs_send.at[0, other], out_recv.at[other], {"px": other}).wait_recv()
        for chunk in range(chunks):
            to_px(chunk, other).wait_send()

    over_px(settle)
    pltpu.make_async_copy(out.at[me], out.at[me], out_recv.at[me]).wait()
    for halo in halos:
        halo.wait_send()
    for step in range(1, npy):
        other = lax.rem(my + step, npy)
        for index in range(len(forward)):
            piece_y(index, other, my).wait_send()
    for side in range(2):
        for step in range(npy):
            other = lax.rem(my + step, npy)
            over_px(lambda other_x: to_cells(side, other, other_x).wait_send())
            if step:
                to_cells(side, other, me).wait_send()


def fused(velocity, forcing, cross_x, cross_y, inv_x, inv_y):
    npx, npy = lax.axis_size("px"), lax.axis_size("py")
    levels, rows, cols = velocity.shape
    part = rows // npy
    half, chunks = part // 2, cols // 128
    wide = cols // chunks
    shape, narrow = velocity.shape, jnp.bfloat16
    order_x, order_y = npx * rows, npy * cols
    vmem, dma = pltpu.VMEM, pltpu.SemaphoreType.DMA
    settled = pl.pallas_call(
        functools.partial(kernel, npx, npy),
        out_shape=jax.ShapeDtypeStruct(shape, narrow),
        in_specs=[pl.BlockSpec(memory_space=pl.ANY)] * 6,
        out_specs=pl.BlockSpec(memory_space=pl.ANY),
        scratch_shapes=[
            vmem(shape, jnp.float32),
            vmem(shape, narrow),
            vmem(shape, narrow),
            vmem(shape, narrow),
            vmem((npx, rows, order_x), narrow),
            vmem((order_y, order_y), narrow),
            vmem((levels, 8, cols), jnp.float32),
            vmem((levels, 8, cols), jnp.float32),
            vmem((2, levels, rows), jnp.float32),
            vmem((2, levels, rows), jnp.float32),
            vmem((levels + 2, rows, cols), jnp.float32),
            vmem((levels + 2, rows, cols), jnp.float32),
            vmem(shape, jnp.float32),
            vmem((chunks, levels, rows, wide), narrow),
            vmem((chunks, npx, rows, wide), narrow),
            vmem((chunks + 1, npy, npx, part, wide), narrow),
            vmem((npx, part, order_y), narrow),
            vmem((2, npy, npx, half, cols), narrow),
            dma((6,)),
            dma((4,)),
            dma((4,)),
            dma((chunks, npx)),
            dma((chunks, npx)),
            dma((chunks + 1, npy)),
            dma((chunks + 1, npy)),
            dma((2, npy, npx)),
            dma((npx,)),
        ],
        compiler_params=pltpu.CompilerParams(collective_id=0, has_side_effects=True, vmem_limit_bytes=56_000_000),
        cost_estimate=pl.CostEstimate(flops=4 * order_x * order_y * rows, bytes_accessed=8 * 1024 * 1024, transcendentals=0),
    )(
        velocity,
        forcing,
        cross_x,
        cross_y,
        inv_x.reshape(npx, rows, order_x),
        inv_y.reshape(order_y, order_y),
    )
    return velocity + settled.astype(jnp.float32)


def step(velocity, forcing, cross_x, cross_y, inv_x, inv_y):
    npx, npy = lax.axis_size("px"), lax.axis_size("py")
    levels, rows, cols = velocity.shape
    aligned = rows % (32 * npy) == 0 and rows % 128 == 0 and cols % 128 == 0 and levels % 8 == 0
    if aligned and levels == npx and levels <= 128 and inv_x.shape[0] == 1:
        return fused(velocity, forcing, cross_x, cross_y, inv_x, inv_y)
    return shards(velocity, forcing, cross_x, cross_y, inv_x, inv_y)


def solution(mesh):
    return jax.shard_map(
        step,
        mesh=mesh,
        in_specs=(
            P(None, "px", "py"),
            P(None, "px", "py"),
            P(None, "px", "py"),
            P(None, "px", "py"),
            P("px", None, None),
            P("px", None, None),
        ),
        out_specs=P(None, "px", "py"),
        check_vma=False,
    )
```
